256 devices in a mesh: date: 64 (over x_hi, z, y), rng: 4 (over x_lo, core).
Axes of the slice: x: 4 (x_hi: 2, x_lo: 2; x = x_hi * 2 + x_lo), y: 4, z: 8, core: 2. Of those that a mesh axis runs over, the one named last changes fastest.
Arguments:
- slc: bfloat16 [64, 2, 64, 4096], P('date', None, None, 'rng'), may hold values from -9 to 9
- ref_date: int32 [1], replicated, may hold values from 0 to 63
- int_offset: int32 [64, 1, 64], P('date', None, 'rng'), may hold values from -4 to 4
- frac_offset: float32 [64, 1, 64], P('date', None, 'rng'), may hold values from 0 to 1
- partners: int32 [64, 4], P('date'), may hold values from 0 to 1, as said below
Outputs:
- surface: float32 [64, 1, 64, 1024], P('date', None, 'rng')
- coherence: bfloat16 [64, 4, 64, 4096], P('date', None, None, 'rng')
The draws below stay inside these ranges and needn't reach their ends.
Inputs may be any that keep to these rules, and one draw needn't show every extreme that they name: `partners`: each row holds 2 to 4 ones.
All inputs are finite; a program needn't handle non-finite values.
Results may differ from the reference program's by a relative error of at most 0.009.
Values may be sent and summed in bfloat16 or wider, within the bound.
A program may use at most 64 MiB of HBM per device.

```python
import jax
import jax.numpy as jnp
from jax import lax

BLK = 64
OVS = 2
LAGS = 32
IMAX = 4
SPAN = 4
BOXA = 5
BOXR = 19
AZ = 64
DATES = 64
NRG = 4096


def shift_table(key):
    table = jax.random.randint(jax.random.fold_in(key, 11), (DATES, AZ // BLK, NRG // BLK), -IMAX, IMAX + 1)
    table = table.at[0, 0, 0].set(IMAX)
    table = table.at[DATES - 1, AZ // BLK - 1, NRG // BLK - 1].set(-IMAX)
    return table.astype(jnp.int32)


def draw_int_offset(key, part):
    return shift_table(key)


def draw_slc(key, part):
    table = shift_table(key)
    width = NRG + 2 * IMAX
    scene = jnp.clip(jax.random.normal(jax.random.fold_in(key, 21), (2, AZ, width), jnp.float32), -6.0, 6.0)
    noise = 0.5 * jnp.clip(jax.random.normal(jax.random.fold_in(key, 22), (DATES, 2, AZ, NRG), jnp.float32), -6.0, 6.0)
    columns = jnp.arange(NRG, dtype=jnp.int32)

    def one_date(pair):
        shifts, extra = pair
        full = jnp.repeat(jnp.repeat(shifts, BLK, axis=0), BLK, axis=1)
        index = columns[None, :] + IMAX - full
        index = jnp.broadcast_to(index[None], (2, AZ, NRG))
        return jnp.take_along_axis(scene, index, axis=2) + extra
    return lax.map(one_date, (table, noise)).astype(jnp.bfloat16)


def draw_partners(key, part):
    counts = jax.random.randint(jax.random.fold_in(key, 31), (DATES, 1), 2, SPAN + 1)
    scores = jax.random.randint(jax.random.fold_in(key, 32), (DATES, SPAN), 0, 1000) * SPAN + jnp.arange(SPAN, dtype=jnp.int32)[None, :]
    ranks = jnp.argsort(jnp.argsort(scores, axis=1), axis=1)
    return (ranks < counts).astype(jnp.int32)


def shard_levels(stream_key, shape, cuts, smallest, high):
    factor_of = 1.0
    for axis_at, parts in cuts:
        steps = jax.random.uniform(jax.random.fold_in(jax.random.fold_in(stream_key, 6), axis_at), (parts,), jnp.float32, smallest / len(cuts), high / len(cuts))
        factor_of = factor_of * jnp.repeat(jnp.exp(steps), shape[axis_at] // parts).reshape((-1,) + (1,) * (len(shape) - 1 - axis_at))
    return factor_of


def setup_inputs(seed: int = 0) -> dict:
    keys = jax.random.split(jax.random.key(seed), 6)
    slc = draw_slc(jax.random.fold_in(keys[5], 71), 0)
    ref_date = jax.random.randint(keys[1], (1,), 0, DATES).astype(jnp.int32)
    int_offset = draw_int_offset(jax.random.fold_in(keys[5], 71), 0)
    frac_offset = jnp.clip(1.0 * jax.random.uniform(keys[3], (DATES, AZ // BLK, NRG // BLK), jnp.float32) ** shard_levels(keys[3], (DATES, AZ // BLK, NRG // BLK), ((0, 64), (2, 4)), -0.2, 0.2), 0.0, 1.0)
    partners = draw_partners(jax.random.fold_in(keys[5], 71), 0)
    return {"slc": slc, "ref_date": ref_date, "int_offset": int_offset, "frac_offset": frac_offset, "partners": partners}


HIGHEST = lax.Precision.HIGHEST

def dft_tables(block, lags, factor):
    index = jnp.arange(block, dtype=jnp.int32)
    phase = index[:, None] * index[None, :] % block
    angle = 2.0 * jnp.pi / block * phase.astype(jnp.float32)
    upsampled = factor * block
    signed = jnp.where(index < block // 2, index, index - block)
    lag_index = jnp.arange(lags, dtype=jnp.int32) - lags // 2
    lag_phase = lag_index[:, None] * signed[None, :] % upsampled
    lag_angle = 2.0 * jnp.pi / upsampled * lag_phase.astype(jnp.float32)
    return (jnp.cos(angle), jnp.sin(angle), jnp.cos(lag_angle), jnp.sin(lag_angle))

def amplitude(slab):
    real_part = slab[0].astype(jnp.float32)
    imag_part = slab[1].astype(jnp.float32)
    return jnp.sqrt(real_part * real_part + imag_part * imag_part + 1e-06).astype(jnp.bfloat16)

def prepare(amplitude_map, block):
    rows, cols = amplitude_map.shape
    blocks = amplitude_map.astype(jnp.float32).reshape(rows // block, block, cols // block, block)
    blocks = blocks.transpose(0, 2, 1, 3)
    centered = blocks - lax.optimization_barrier(jnp.mean(blocks, axis=(2, 3), keepdims=True))
    energy = lax.optimization_barrier(jnp.sum(centered * centered, axis=(2, 3)))
    return (centered, energy)

def spectra(centered, cosine, sine):
    first_real = jnp.einsum('kn,abnm->abkm', cosine, centered, precision=HIGHEST)
    first_imag = -jnp.einsum('kn,abnm->abkm', sine, centered, precision=HIGHEST)
    real_part = jnp.einsum('abkn,ln->abkl', first_real, cosine, precision=HIGHEST) + jnp.einsum('abkn,ln->abkl', first_imag, sine, precision=HIGHEST)
    imag_part = jnp.einsum('abkn,ln->abkl', first_imag, cosine, precision=HIGHEST) - jnp.einsum('abkn,ln->abkl', first_real, sine, precision=HIGHEST)
    return (real_part, imag_part)

def correlate(own_amplitude, ref_amplitude):
    cosine, sine, lag_cos, lag_sin = dft_tables(BLK, LAGS, OVS)
    own_blocks, own_energy = prepare(own_amplitude, BLK)
    ref_blocks, ref_energy = prepare(ref_amplitude, BLK)
    own_real, own_imag = spectra(own_blocks, cosine, sine)
    ref_real, ref_imag = spectra(ref_blocks, cosine, sine)
    cross_real = own_real * ref_real + own_imag * ref_imag
    cross_imag = own_imag * ref_real - own_real * ref_imag
    left_real = jnp.einsum('mk,abkl->abml', lag_cos, cross_real, precision=HIGHEST) - jnp.einsum('mk,abkl->abml', lag_sin, cross_imag, precision=HIGHEST)
    left_imag = jnp.einsum('mk,abkl->abml', lag_cos, cross_imag, precision=HIGHEST) + jnp.einsum('mk,abkl->abml', lag_sin, cross_real, precision=HIGHEST)
    values = jnp.einsum('abml,nl->abmn', left_real, lag_cos, precision=HIGHEST) - jnp.einsum('abml,nl->abmn', left_imag, lag_sin, precision=HIGHEST)
    scale = BLK * jnp.sqrt(own_energy * ref_energy + 1e-06)
    values = values / scale[:, :, None, None]
    return values.reshape(values.shape[0], values.shape[1], LAGS * LAGS)

def resample(padded, shifts, fractions, block, rim):
    block_rows, block_cols = shifts.shape
    row_start = jnp.broadcast_to((jnp.arange(block_rows, dtype=jnp.int32) * block)[:, None], (block_rows, block_cols)).reshape(-1)
    col_start = ((jnp.arange(block_cols, dtype=jnp.int32) * block)[None, :] + shifts.astype(jnp.int32) + (rim - 3)).reshape(-1)
    anchor = jnp.zeros((), jnp.int32)

    def tile(row, col):
        return lax.dynamic_slice(padded, (anchor, row, col), (2, block, block + 7))
    tiles = jax.vmap(tile)(row_start, col_start)
    distance = jnp.arange(8, dtype=jnp.float32)[None, :] - 3.0 - fractions.reshape(-1)[:, None]
    weights = jnp.sinc(distance) * (0.5 + 0.5 * jnp.cos(jnp.pi * distance / 4.0))
    result = weights[:, 0, None, None, None] * tiles[..., 0:block].astype(jnp.float32)
    for tap in range(1, 8):
        result = result + weights[:, tap, None, None, None] * tiles[..., tap:tap + block].astype(jnp.float32)
    result = result.reshape(block_rows, block_cols, 2, block, block).transpose(2, 0, 3, 1, 4)
    return result.reshape(2, block_rows * block, block_cols * block).astype(jnp.bfloat16)

def boxcar(field, box_rows, box_cols):
    half = box_rows // 2
    padded = jnp.pad(field, ((half, half), (0, 0)))
    rows = field.shape[0]
    summed = padded[0:rows]
    for offset in range(1, box_rows):
        summed = summed + padded[offset:offset + rows]
    width = field.shape[1] - (box_cols - 1)
    total = summed[:, 0:width]
    for offset in range(1, box_cols):
        total = total + summed[:, offset:offset + width]
    return total

def coherence_map(own_ext, partner_ext, weight):
    own_real = own_ext[0].astype(jnp.float32)
    own_imag = own_ext[1].astype(jnp.float32)
    other_real = partner_ext[0].astype(jnp.float32)
    other_imag = partner_ext[1].astype(jnp.float32)
    box_re = boxcar(own_real * other_real + own_imag * other_imag, BOXA, BOXR)
    box_im = boxcar(own_imag * other_real - own_real * other_imag, BOXA, BOXR)
    box_own = boxcar(own_real * own_real + own_imag * own_imag, BOXA, BOXR)
    box_partner = boxcar(other_real * other_real + other_imag * other_imag, BOXA, BOXR)
    value = weight.astype(jnp.float32) * (box_re * box_re + box_im * box_im) / (box_own * box_partner + 1e-06)
    return value.astype(jnp.bfloat16)

def reference(slc, ref_date, int_offset, frac_offset, partners):
    amplitudes = lax.map(amplitude, slc)
    ref_amplitude = lax.dynamic_index_in_dim(amplitudes, ref_date[0], 0, keepdims=False)
    surfaces = lax.map(lambda own: correlate(own, ref_amplitude), amplitudes)
    rim = IMAX + 4

    def resample_date(triple):
        slab, shifts, fractions = triple
        padded = jnp.pad(slab, ((0, 0), (0, 0), (rim, rim)))
        return resample(padded, shifts, fractions, BLK, rim)
    resampled = lax.map(resample_date, (slc, int_offset, frac_offset))
    half = BOXR // 2
    extended = jnp.pad(resampled, ((0, 0), (0, 0), (0, 0), (half, half)))
    results = []
    for ahead in range(1, SPAN + 1):
        partner = jnp.concatenate([extended[ahead:], jnp.zeros_like(extended[:ahead])], axis=0)
        results.append(lax.map(lambda triple: coherence_map(triple[0], triple[1], triple[2]), (extended, partner, partners[:, ahead - 1])))
    return (surfaces, jnp.stack(results, axis=1))
```

```python
import functools

import jax
import jax.numpy as jnp
import numpy as np
from jax import lax
from jax.experimental import pallas as pl
from jax.experimental.pallas import tpu as pltpu
from jax.sharding import PartitionSpec as P

BLK = 64
LAGS = 32
SPAN = 4
NY = 4
TILES = 8
ROWS = 64
LANES = 128
MESH = pl.DeviceIdType.MESH
F32 = jnp.float32
BF16 = jnp.bfloat16

RIGHT, LEFT, VRIGHT, VLEFT, COLS, LINES, TABLE_ROWS = 0, 128, 256, 512, 544, 1056, 1248


def tables():
    n = np.arange(BLK)
    angle = 2.0 * np.pi / BLK * (n[:, None] * n[None, :] % BLK)
    cosine, sine = np.cos(angle), np.sin(angle)
    signed = np.where(n < BLK // 2, n, n - BLK)
    lag = np.arange(LAGS) - LAGS // 2
    lag_angle = 2.0 * np.pi / (2 * BLK) * (lag[:, None] * signed[None, :] % (2 * BLK))
    lag_cos, lag_sin = np.cos(lag_angle), np.sin(lag_angle)
    table = np.zeros((TABLE_ROWS, 256), np.float64)
    for b in range(2):
        rows = slice(RIGHT + 64 * b, RIGHT + 64 * b + 64)
        table[rows, 64 * b : 64 * b + 64] = cosine
        table[rows, 128 + 64 * b : 128 + 64 * b + 64] = sine
        top = VRIGHT + 128 * b
        table[top + 64 * b : top + 64 * b + 64, 0:128] = np.tile(lag_cos.T, (1, 4))
        table[top + 64 * b : top + 64 * b + 64, 128:256] = np.tile(lag_sin.T, (1, 4))
    table[LEFT : LEFT + 64, 0:64] = cosine
    table[LEFT : LEFT + 64, 64:128] = -sine
    table[LEFT + 64 : LEFT + 128, 0:64] = -sine
    table[LEFT + 64 : LEFT + 128, 64:128] = -cosine
    order = np.array([4 * q + i for i in range(4) for q in range(8)])
    table[VLEFT : VLEFT + 32] = np.concatenate([lag_cos, -lag_sin, -lag_sin, -lag_cos], axis=1)[order]
    c, r = np.arange(512)[:, None], np.arange(256)[None, :]
    table[COLS : COLS + 512] = np.abs(c - 128 - r) <= 9
    c, r = np.arange(192)[:, None], np.arange(192)[None, :]
    table[LINES : LINES + 192, 0:192] = (np.abs(c - r) <= 2) & (c // 64 == r // 64)
    return jnp.asarray(table, BF16)


def tap_rows(off_s, frac_s):
    row = lax.broadcasted_iota(jnp.int32, (16, LANES), 0)
    lane = lax.broadcasted_iota(jnp.int32, (16, LANES), 1)
    off = jnp.zeros((16, LANES), jnp.int32)
    frac = jnp.zeros((16, LANES), F32)
    for j in range(16):
        off = jnp.where(row == j, off_s[0, 0, j], off)
        frac = jnp.where(row == j, frac_s[0, 0, j], frac)
    u = jnp.where(lane < 64, -lane, 128 - lane) - off
    valid = (u >= -3) & (u <= 4)
    uf = u.astype(F32)
    x = uf - frac
    near = jnp.minimum(frac, 1.0 - frac)
    a = near * np.float32(np.pi)
    a2 = a * a
    series = np.float32(1.6059044e-10)
    for coefficient in (-2.5052108e-8, 2.7557319e-6, -1.9841270e-4, 8.3333333e-3, -1.6666667e-1, 1.0):
        series = series * a2 + np.float32(coefficient)
    sine = a * series
    sign = jnp.where((u & 1) == 0, -1.0, 1.0)
    zero = x == 0.0
    sinc = jnp.where(zero, 1.0, sign * sine / jnp.where(zero, 1.0, np.float32(np.pi) * x))
    b = x * np.float32(np.pi / 8)
    b2 = b * b
    half = np.float32(-1.1470746e-11)
    for coefficient in (2.0876757e-9, -2.7557319e-7, 2.4801587e-5, -1.3888889e-3, 4.1666667e-2, -0.5, 1.0):
        half = half * b2 + np.float32(coefficient)
    return jnp.where(valid, sinc * half * half, 0.0)


def resample_tile(s, samples, first, second, lane, diff):
    first = jnp.broadcast_to(first, (LANES, LANES))
    second = jnp.broadcast_to(second, (LANES, LANES))
    first = pltpu.roll(first, 0, 1, stride=1, stride_axis=0)
    second = pltpu.roll(second, 0, 1, stride=1, stride_axis=0)
    band = jnp.where(lane < 64, first, second)
    high = band.astype(BF16).astype(F32)
    low = band - high
    parts = []
    for keep in (diff >= 64, jnp.abs(diff) < 64, diff <= -64):
        parts.append(
            jnp.concatenate(
                [jnp.where(keep, high, 0.0).astype(BF16), jnp.where(keep, low, 0.0).astype(BF16)], axis=1
            )
        )
    weights = jnp.concatenate(parts, axis=0)
    window = jnp.concatenate(
        [samples[i].reshape(128, LANES) for i in ((s + 8) % 9, s, (s + 1) % 9)], axis=1
    )
    both = jnp.dot(window, weights, preferred_element_type=F32)
    return both[:, 0:LANES] + both[:, LANES:256]


def halves(rows, lane):
    left = jnp.sum(jnp.where(lane < 64, rows, 0.0), axis=1, keepdims=True)
    right = jnp.sum(jnp.where(lane < 64, 0.0, rows), axis=1, keepdims=True)
    return jnp.where(lane < 64, left, right)


def spectrum(amp, table, lane8):
    blocks = [amp[p].astype(F32) for p in range(TILES)]
    sums = jnp.concatenate([jnp.sum(b, axis=0, keepdims=True) for b in blocks], axis=0)
    mean = halves(sums, lane8) * np.float32(1.0 / (BLK * BLK))
    centered = [b - mean[p : p + 1] for p, b in enumerate(blocks)]
    squares = jnp.concatenate([jnp.sum(c * c, axis=0, keepdims=True) for c in centered], axis=0)
    energy = halves(squares, lane8)
    stacked = jnp.concatenate([c.astype(BF16) for c in centered], axis=0)
    along = jnp.dot(stacked, table[RIGHT : RIGHT + 128, :], preferred_element_type=F32)
    left = table[LEFT : LEFT + 128, 0:128]
    out = []
    for p in range(TILES):
        part = along[64 * p : 64 * p + 64]
        part = jnp.concatenate([part[:, 0:128], part[:, 128:256]], axis=0).astype(BF16)
        out.append(jnp.dot(left, part, preferred_element_type=F32))
    return out, energy


def surfaces(own_spec, own_energy, ref_parts, ref_energy, table, out, lane8):
    scale = 1.0 / (np.float32(BLK) * jnp.sqrt(own_energy * ref_energy + 1e-06))
    vleft = table[VLEFT : VLEFT + 32, :]
    for p in range(TILES):
        own_real, own_imag = own_spec[p, 0:64], own_spec[p, 64:128]
        ref_real, ref_imag = ref_parts[p][0:64], ref_parts[p][64:128]
        cross = jnp.concatenate(
            [own_real * ref_real + own_imag * ref_imag, own_imag * ref_real - own_real * ref_imag], axis=0
        ).astype(BF16)
        for b in range(2):
            right = table[VRIGHT + 128 * b : VRIGHT + 128 * b + 128, :]
            turned = jnp.dot(cross, right, preferred_element_type=F32)
            turned = jnp.concatenate([turned[:, 0:128], turned[:, 128:256]], axis=0).astype(BF16)
            value = jnp.dot(vleft, turned, preferred_element_type=F32)
            picked = value[0:8]
            for i in range(1, 4):
                picked = jnp.where(lane8 >= 32 * i, value[8 * i : 8 * i + 8], picked)
            picked = picked * jnp.broadcast_to(scale[p : p + 1, 64 * b : 64 * b + 1], (8, LANES))
            out[2 * p + b] = picked


def box_group(g, fields, rows, table, lines):
    window = jnp.concatenate(
        [fields[i, 0:rows] for i in ((2 * g + 8) % 9, 2 * g, 2 * g + 1, 2 * g + 2)], axis=1
    )
    summed = jnp.dot(window, table[COLS : COLS + 512, :], preferred_element_type=F32)
    return jnp.dot(lines, summed.astype(BF16), preferred_element_type=F32)


def kernel(
    nz, nx, nr,
    ref_s, off_s, frac_s, part_s, slc_h, table_h,
    surf_h, coh_h,
    table, samples, halo, taps, tap_halo, amp, masked, scatter, merged, exchange, ref_amp,
    own_spec, own, partner, fields, box_own, coh, surf,
    in_sem, halo_send, halo_recv, rs_send, rs_recv, ae_send, ae_recv, ag_send, ag_recv,
    own_send, relay_send, item_recv, out_sem,
):
    date, rng = lax.axis_index("date"), lax.axis_index("rng")
    planes = nx * nz
    nxy = nx * NY
    ts = TILES // nz
    plane, y = date // NY, date % NY
    z, xy = plane % nz, (plane // nz) * NY + y
    has_left, has_right = rng > 0, rng < nr - 1
    has_before, has_after = plane > 0, plane < planes - 1

    def z_date(k):
        return ((plane // nz) * nz + (z + k) % nz) * NY + y

    def xy_date(k):
        other = (xy + k) % nxy
        return ((other // NY) * nz + z) * NY + other % NY

    def remote(src, dst, send, recv, to_date, to_rng):
        return pltpu.make_async_remote_copy(
            src_ref=src, dst_ref=dst, send_sem=send, recv_sem=recv,
            device_id=(to_date, to_rng), device_id_type=MESH,
        )

    loads = [
        pltpu.make_async_copy(slc_h.at[0, :, :, pl.ds(128 * p, 128)], samples.at[p], in_sem.at[p])
        for p in range(TILES)
    ]
    for load in loads:
        load.start()
    table_load = pltpu.make_async_copy(table_h, table, in_sem.at[TILES])
    table_load.start()

    barrier = pltpu.get_barrier_semaphore()

    def hello(to_date, to_rng):
        pl.semaphore_signal(barrier, inc=1, device_id=(to_date, to_rng), device_id_type=MESH)

    for k in range(1, nz):
        hello(z_date(k), rng)
    for k in range(1, nxy):
        hello(xy_date(k), rng)
    for present, to_date, to_rng in (
        (has_left, date, rng - 1), (has_right, date, rng + 1),
        (has_before, date - NY, rng), (has_after, date + NY, rng),
    ):
        @pl.when(present)
        def _(to_date=to_date, to_rng=to_rng):
            hello(to_date, to_rng)

    lane = lax.broadcasted_iota(jnp.int32, (LANES, LANES), 1)
    diff = lax.broadcasted_iota(jnp.int32, (LANES, LANES), 0) - lane
    lane8 = lane[0:8]
    rows = tap_rows(off_s, frac_s)
    taps[...] = rows

    @pl.when(jnp.logical_not(has_left))
    def _():
        halo[0] = jnp.zeros((2, ROWS, LANES), BF16)
        tap_halo[0] = jnp.zeros((8, LANES), F32)

    @pl.when(jnp.logical_not(has_right))
    def _():
        halo[1] = jnp.zeros((2, ROWS, LANES), BF16)
        tap_halo[1] = jnp.zeros((8, LANES), F32)

    for h in range(1, SPAN + 1):
        @pl.when(jnp.logical_not(jnp.logical_or(y + h < NY, has_after)))
        def _(h=h):
            partner[h - 1] = jnp.zeros((9, 2, ROWS, LANES), BF16)

    root = jnp.where(ref_s[0] == date, 1.0, 0.0).astype(F32)
    for p in range(TILES):
        loads[p].wait()
        real, imag = samples[p, 0].astype(F32), samples[p, 1].astype(F32)
        size = jnp.sqrt(real * real + imag * imag + 1e-06).astype(BF16)
        amp[p] = size
        masked[p] = (size.astype(F32) * root).astype(BF16)

    greeted = (nz - 1) + (nxy - 1)
    for present in (has_left, has_right, has_before, has_after):
        greeted = greeted + present.astype(jnp.int32)
    pl.semaphore_wait(barrier, greeted)

    scatters = []
    for k in range(1, nz):
        to = (z + k) % nz
        scatters.append(
            remote(masked.at[pl.ds(to * ts, ts)], scatter.at[k - 1], rs_send.at[k - 1], rs_recv.at[k - 1],
                   z_date(k), rng)
        )
    to_left = [
        remote(samples.at[0], halo.at[1], halo_send.at[0], halo_recv.at[0], date, rng - 1),
        remote(taps.at[pl.ds(0, 8)], tap_halo.at[1], halo_send.at[1], halo_recv.at[1], date, rng - 1),
    ]
    to_right = [
        remote(samples.at[7], halo.at[0], halo_send.at[2], halo_recv.at[2], date, rng + 1),
        remote(taps.at[pl.ds(8, 8)], tap_halo.at[0], halo_send.at[3], halo_recv.at[3], date, rng + 1),
    ]

    @pl.when(has_left)
    def _():
        for copy in to_left:
            copy.start()

    @pl.when(has_right)
    def _():
        for copy in to_right:
            copy.start()

    for copy in scatters:
        copy.start()

    chunks = ((1, 6), (7, 2), (0, 1))
    nc = len(chunks)

    def item_copies(source, c, slot, send, to_date):
        start, count = chunks[c]
        return remote(
            source.at[pl.ds(start, count)], partner.at[slot, pl.ds(start, count)],
            send, item_recv.at[slot, c], to_date, rng,
        )

    own_dests = [(has_before, SPAN - 1, date - NY)] + [(y >= k, k - 1, date - k) for k in range(1, NY)]
    own_copies = [
        [item_copies(own, c, slot, own_send.at[i, c], to) for c in range(nc)]
        for i, (_, slot, to) in enumerate(own_dests)
    ]
    relay_dests = [
        (jnp.logical_and(has_after, y + k < NY), SPAN - k - 1, date + k) for k in range(1, NY)
    ]
    relay_copies = [
        [item_copies(partner.at[SPAN - 1], c, slot, relay_send.at[i, c], to) for c in range(nc)]
        for i, (_, slot, to) in enumerate(relay_dests)
    ]

    def send_own(c):
        for (present, _, _), copies in zip(own_dests, own_copies):
            @pl.when(present)
            def _(copies=copies):
                copies[c].start()

    def store_own(s, keep=None):
        if s < TILES:
            first, second = rows[2 * s : 2 * s + 1], rows[2 * s + 1 : 2 * s + 2]
        else:
            first, second = tap_halo[1][0:1], tap_halo[0][7:8]
        tile = resample_tile(s, samples, first, second, lane, diff)
        if keep is not None:
            tile = jnp.where(keep, tile, 0.0)
        own[s] = tile.astype(BF16).reshape(2, ROWS, LANES)

    for s in range(1, 7):
        store_own(s)
    send_own(0)

    @pl.when(has_right)
    def _():
        to_left[0].wait_recv()
        to_left[1].wait_recv()

    @pl.when(has_left)
    def _():
        to_right[0].wait_recv()
        to_right[1].wait_recv()

    lane_h = lax.broadcasted_iota(jnp.int32, (2, ROWS, LANES), 2)
    samples[8] = jnp.where(lane_h < 64, halo[1].astype(F32), halo[0].astype(F32)).astype(BF16)
    low_edge = jnp.where(has_right, 64, 0)
    high_edge = jnp.where(has_left, 64, 128)
    store_own(7)
    store_own(8, jnp.logical_or(lane < low_edge, lane >= high_edge))
    send_own(1)
    store_own(0)
    send_own(2)

    table_load.wait()
    parts, own_energy = spectrum(amp, table, lane8)
    for p in range(TILES):
        own_spec[p] = parts[p]

    for copy in scatters:
        copy.wait_recv()
    total = masked[pl.ds(z * ts, ts)].astype(F32)
    for k in range(nz - 1):
        total = total + scatter[k].astype(F32)
    merged[...] = total.astype(BF16)
    exchanges = [
        remote(merged, exchange.at[k - 1], ae_send.at[k - 1], ae_recv.at[k - 1], xy_date(k), rng)
        for k in range(1, nxy)
    ]
    for copy in exchanges:
        copy.start()

    lines = table[LINES : LINES + 192, 0:192]
    for s in range(9):
        real, imag = own[s, 0].astype(F32), own[s, 1].astype(F32)
        fields[s, 0:64] = (real * real + imag * imag).astype(BF16)
    for g in range(4):
        box_own[:, 256 * g : 256 * g + 256] = box_group(g, fields, 64, table, table[LINES : LINES + 64, 0:64])

    for c in range(nc):
        @pl.when(has_after)
        def _(c=c):
            own_copies[0][c].wait_recv()

        for (present, _, _), copies in zip(relay_dests, relay_copies):
            @pl.when(present)
            def _(copies=copies):
                copies[c].start()

    outs = []

    def pair(h):
        slot = h - 1
        if h < SPAN:
            @pl.when(jnp.logical_or(y + h < NY, has_after))
            def _():
                for c in range(nc):
                    own_copies[h][c].wait_recv()
        for s in range(9):
            own0, own1 = own[s, 0].astype(F32), own[s, 1].astype(F32)
            other0, other1 = partner[slot, s, 0].astype(F32), partner[slot, s, 1].astype(F32)
            fields[s, 0:64] = (own0 * other0 + own1 * other1).astype(BF16)
            fields[s, 64:128] = (own1 * other0 - own0 * other1).astype(BF16)
            fields[s, 128:192] = (other0 * other0 + other1 * other1).astype(BF16)
        weight = part_s[0, slot].astype(F32)
        for g in range(4):
            box = box_group(g, fields, 192, table, lines)
            re, im, power = box[0:64], box[64:128], box[128:192]
            mine = box_own[:, 256 * g : 256 * g + 256]
            value = weight * (re * re + im * im) / (mine * power + 1e-06)
            coh[slot, :, 256 * g : 256 * g + 256] = value.astype(BF16)
        out = pltpu.make_async_copy(coh.at[slot], coh_h.at[0, slot], out_sem.at[slot])
        out.start()
        outs.append(out)

    pair(4)

    for copy in exchanges:
        copy.wait_recv()
    total = merged[...].astype(F32)
    for k in range(nxy - 1):
        total = total + exchange[k].astype(F32)
    ref_amp[pl.ds(z * ts, ts)] = total.astype(BF16)
    mine = ref_amp.at[pl.ds(z * ts, ts)]
    gathers = [
        remote(mine, mine, ag_send.at[k - 1], ag_recv.at[k - 1], z_date(k), rng) for k in range(1, nz)
    ]
    for copy in gathers:
        copy.start()

    pair(1)
    pair(2)

    for copy in gathers:
        copy.wait_recv()
    ref_parts, ref_energy = spectrum(ref_amp, table, lane8)
    surfaces(own_spec, own_energy, ref_parts, ref_energy, table, surf, lane8)
    out = pltpu.make_async_copy(surf, surf_h.at[0, 0], out_sem.at[SPAN])
    out.start()
    outs.append(out)

    pair(3)

    for copy in scatters + exchanges + gathers:
        copy.wait_send()

    @pl.when(has_left)
    def _():
        for copy in to_left:
            copy.wait_send()

    @pl.when(has_right)
    def _():
        for copy in to_right:
            copy.wait_send()

    for dests, copies in ((own_dests, own_copies), (relay_dests, relay_copies)):
        for (present, _, _), mine in zip(dests, copies):
            @pl.when(present)
            def _(mine=mine):
                for copy in mine:
                    copy.wait_send()
    for out in outs:
        out.wait()


def body(nz, nx, nr, slc, ref_date, int_offset, frac_offset, partners):
    ts = TILES // nz
    nxy = nx * NY
    smem = pl.BlockSpec(memory_space=pltpu.SMEM)
    anywhere = pl.BlockSpec(memory_space=pl.ANY)
    dma = pltpu.SemaphoreType.DMA
    tile = (2, ROWS, LANES)
    slab = (TILES, ROWS, LANES)
    surface, coherence = pl.pallas_call(
        functools.partial(kernel, nz, nx, nr),
        out_shape=(
            jax.ShapeDtypeStruct((1, 1, 16, 8, LANES), F32),
            jax.ShapeDtypeStruct((1, SPAN, ROWS, TILES * LANES), BF16),
        ),
        in_specs=[smem, smem, smem, smem, anywhere, anywhere],
        out_specs=(anywhere, anywhere),
        scratch_shapes=[
            pltpu.VMEM((TABLE_ROWS, 256), BF16),
            pltpu.VMEM((9,) + tile, BF16),
            pltpu.VMEM((2,) + tile, BF16),
            pltpu.VMEM((16, LANES), F32),
            pltpu.VMEM((2, 8, LANES), F32),
            pltpu.VMEM(slab, BF16),
            pltpu.VMEM(slab, BF16),
            pltpu.VMEM((max(nz - 1, 1), ts, ROWS, LANES), BF16),
            pltpu.VMEM((ts, ROWS, LANES), BF16),
            pltpu.VMEM((nxy - 1, ts, ROWS, LANES), BF16),
            pltpu.VMEM(slab, BF16),
            pltpu.VMEM((TILES, 128, LANES), F32),
            pltpu.VMEM((9,) + tile, BF16),
            pltpu.VMEM((SPAN, 9) + tile, BF16),
            pltpu.VMEM((9, 192, LANES), BF16),
            pltpu.VMEM((ROWS, TILES * LANES), F32),
            pltpu.VMEM((SPAN, ROWS, TILES * LANES), BF16),
            pltpu.VMEM((16, 8, LANES), F32),
            dma((TILES + 1,)),
            dma((4,)), dma((4,)),
            dma((max(nz - 1, 1),)), dma((max(nz - 1, 1),)),
            dma((nxy - 1,)), dma((nxy - 1,)),
            dma((max(nz - 1, 1),)), dma((max(nz - 1, 1),)),
            dma((4, 3)), dma((3, 3)), dma((4, 3)),
            dma((SPAN + 1,)),
        ],
        compiler_params=pltpu.CompilerParams(collective_id=0, has_side_effects=True),
    )(ref_date, int_offset, frac_offset, partners, slc, tables())
    return surface.reshape(1, 1, 16, 1024), coherence


def solution(mesh):
    dates, nr = mesh.shape["date"], mesh.shape["rng"]
    planes = dates // NY
    nz = min(planes, 8)
    in_specs = (
        P("date", None, None, "rng"),
        P(),
        P("date", None, "rng"),
        P("date", None, "rng"),
        P("date", None),
    )
    out_specs = (P("date", None, "rng", None), P("date", None, None, "rng"))
    return jax.shard_map(
        functools.partial(body, nz, planes // nz, nr),
        mesh=mesh, in_specs=in_specs, out_specs=out_specs, check_vma=False,
    )
```

```python
import functools

import jax
import jax.numpy as jnp
import numpy as np
from jax import lax
from jax.experimental import pallas as pl
from jax.experimental.pallas import tpu as pltpu
from jax.sharding import PartitionSpec as P

BLK = 64
LAGS = 32
SPAN = 4
NY = 4
TILES = 8
ROWS = 64
LANES = 128
MESH = pl.DeviceIdType.MESH
F32 = jnp.float32
BF16 = jnp.bfloat16

RIGHT, LEFT, VRIGHT, VLEFT, COLS, LINES, TABLE_ROWS = 0, 128, 256, 512, 544, 1056, 1248


def tables():
    n = np.arange(BLK)
    angle = 2.0 * np.pi / BLK * (n[:, None] * n[None, :] % BLK)
    cosine, sine = np.cos(angle), np.sin(angle)
    signed = np.where(n < BLK // 2, n, n - BLK)
    lag = np.arange(LAGS) - LAGS // 2
    lag_angle = 2.0 * np.pi / (2 * BLK) * (lag[:, None] * signed[None, :] % (2 * BLK))
    lag_cos, lag_sin = np.cos(lag_angle), np.sin(lag_angle)
    table = np.zeros((TABLE_ROWS, 256), np.float64)
    for b in range(2):
        rows = slice(RIGHT + 64 * b, RIGHT + 64 * b + 64)
        table[rows, 64 * b : 64 * b + 64] = cosine
        table[rows, 128 + 64 * b : 128 + 64 * b + 64] = sine
        rows = slice(VRIGHT + 64 * b, VRIGHT + 64 * b + 64)
        table[rows, 128 * b : 128 * b + 128] = np.tile(lag_cos.T, (1, 4))
        rows = slice(VRIGHT + 128 + 64 * b, VRIGHT + 128 + 64 * b + 64)
        table[rows, 128 * b : 128 * b + 128] = np.tile(lag_sin.T, (1, 4))
    table[LEFT : LEFT + 64, 0:64] = cosine
    table[LEFT : LEFT + 64, 64:128] = -sine
    table[LEFT + 64 : LEFT + 128, 0:64] = -sine
    table[LEFT + 64 : LEFT + 128, 64:128] = -cosine
    order = np.array([4 * q + i for i in range(4) for q in range(8)])
    table[VLEFT : VLEFT + 32] = np.concatenate([lag_cos, -lag_sin, -lag_sin, -lag_cos], axis=1)[order]
    c, r = np.arange(512)[:, None], np.arange(256)[None, :]
    table[COLS : COLS + 512] = np.abs(c - 128 - r) <= 9
    c, r = np.arange(192)[:, None], np.arange(192)[None, :]
    table[LINES : LINES + 192, 0:192] = (np.abs(c - r) <= 2) & (c // 64 == r // 64)
    return jnp.asarray(table, BF16)


def tap_rows(off_s, frac_s):
    row = lax.broadcasted_iota(jnp.int32, (16, LANES), 0)
    lane = lax.broadcasted_iota(jnp.int32, (16, LANES), 1)
    off = jnp.zeros((16, LANES), jnp.int32)
    frac = jnp.zeros((16, LANES), F32)
    for j in range(16):
        off = jnp.where(row == j, off_s[0, 0, j], off)
        frac = jnp.where(row == j, frac_s[0, 0, j], frac)
    u = jnp.where(lane < 64, -lane, 128 - lane) - off
    valid = (u >= -3) & (u <= 4)
    uf = u.astype(F32)
    x = uf - frac
    near = jnp.minimum(frac, 1.0 - frac)
    a = near * np.float32(np.pi)
    a2 = a * a
    series = np.float32(1.6059044e-10)
    for coefficient in (-2.5052108e-8, 2.7557319e-6, -1.9841270e-4, 8.3333333e-3, -1.6666667e-1, 1.0):
        series = series * a2 + np.float32(coefficient)
    sine = a * series
    sign = jnp.where((u & 1) == 0, -1.0, 1.0)
    zero = x == 0.0
    sinc = jnp.where(zero, 1.0, sign * sine / jnp.where(zero, 1.0, np.float32(np.pi) * x))
    b = x * np.float32(np.pi / 8)
    b2 = b * b
    half = np.float32(-1.1470746e-11)
    for coefficient in (2.0876757e-9, -2.7557319e-7, 2.4801587e-5, -1.3888889e-3, 4.1666667e-2, -0.5, 1.0):
        half = half * b2 + np.float32(coefficient)
    return jnp.where(valid, sinc * half * half, 0.0)


def resample_tile(s, samples, first, second, lane, diff):
    first = jnp.broadcast_to(first, (LANES, LANES))
    second = jnp.broadcast_to(second, (LANES, LANES))
    first = pltpu.roll(first, 0, 1, stride=1, stride_axis=0)
    second = pltpu.roll(second, 0, 1, stride=1, stride_axis=0)
    band = jnp.where(lane < 64, first, second)
    high = band.astype(BF16).astype(F32)
    low = band - high
    parts = []
    for keep in (diff >= 64, jnp.abs(diff) < 64, diff <= -64):
        parts.append(
            jnp.concatenate(
                [jnp.where(keep, high, 0.0).astype(BF16), jnp.where(keep, low, 0.0).astype(BF16)], axis=1
            )
        )
    weights = jnp.concatenate(parts, axis=0)
    window = jnp.concatenate(
        [samples[i].reshape(128, LANES) for i in ((s + 8) % 9, s, (s + 1) % 9)], axis=1
    )
    both = jnp.dot(window, weights, preferred_element_type=F32)
    return both[:, 0:LANES] + both[:, LANES:256]


def halves(rows, lane):
    left = jnp.sum(jnp.where(lane < 64, rows, 0.0), axis=1, keepdims=True)
    right = jnp.sum(jnp.where(lane < 64, 0.0, rows), axis=1, keepdims=True)
    return jnp.where(lane < 64, left, right)


def spectrum(amp, table, lane8):
    blocks = [amp[p].astype(F32) for p in range(TILES)]
    sums = jnp.concatenate([jnp.sum(b, axis=0, keepdims=True) for b in blocks], axis=0)
    mean = halves(sums, lane8) * np.float32(1.0 / (BLK * BLK))
    centered = [b - mean[p : p + 1] for p, b in enumerate(blocks)]
    squares = jnp.concatenate([jnp.sum(c * c, axis=0, keepdims=True) for c in centered], axis=0)
    energy = halves(squares, lane8)
    stacked = jnp.concatenate([c.astype(BF16) for c in centered], axis=0)
    along = jnp.dot(stacked, table[RIGHT : RIGHT + 128, :], preferred_element_type=F32)
    left = table[LEFT : LEFT + 128, 0:128]
    out = []
    for p in range(TILES):
        part = along[64 * p : 64 * p + 64]
        part = jnp.concatenate([part[:, 0:128], part[:, 128:256]], axis=0).astype(BF16)
        out.append(jnp.dot(left, part, preferred_element_type=F32))
    return out, energy


def surfaces(own_spec, own_energy, ref_parts, ref_energy, table, out, lane8):
    scale = 1.0 / (np.float32(BLK) * jnp.sqrt(own_energy * ref_energy + 1e-06))
    vleft = table[VLEFT : VLEFT + 32, :]
    for p in range(TILES):
        own_real, own_imag = own_spec[p, 0:64], own_spec[p, 64:128]
        ref_real, ref_imag = ref_parts[p][0:64], ref_parts[p][64:128]
        cross = jnp.concatenate(
            [own_real * ref_real + own_imag * ref_imag, own_imag * ref_real - own_real * ref_imag], axis=0
        ).astype(BF16)
        turned = [
            jnp.dot(cross, table[top : top + 128, :], preferred_element_type=F32).astype(BF16)
            for top in (VRIGHT, VRIGHT + 128)
        ]
        value = jnp.dot(vleft, jnp.concatenate(turned, axis=0), preferred_element_type=F32)
        for b in range(2):
            half = value[:, 128 * b : 128 * b + 128]
            picked = half[0:8]
            for i in range(1, 4):
                picked = jnp.where(lane8 >= 32 * i, half[8 * i : 8 * i + 8], picked)
            out[2 * p + b] = picked * jnp.broadcast_to(scale[p : p + 1, 64 * b : 64 * b + 1], (8, LANES))


def box_group(g, fields, rows, table, lines):
    window = jnp.concatenate(
        [fields[i, 0:rows] for i in ((2 * g + 8) % 9, 2 * g, 2 * g + 1, 2 * g + 2)], axis=1
    )
    summed = jnp.dot(window, table[COLS : COLS + 512, :], preferred_element_type=F32)
    return jnp.dot(lines, summed.astype(BF16), preferred_element_type=F32)


def kernel(
    nz, nx, nr,
    ref_s, off_s, frac_s, part_s, slc_h, table_h,
    surf, coh,
    table, samples, halo, taps, tap_halo, amp, masked, scatter, merged, exchange, ref_amp,
    own_spec, own, partner, fields, box_own,
    in_sem, halo_send, halo_recv, rs_send, rs_recv, ae_send, ae_recv, ag_send, ag_recv,
    own_send, relay_send, item_recv,
):
    date, rng = lax.axis_index("date"), lax.axis_index("rng")
    planes = nx * nz
    nxy = nx * NY
    ts = TILES // nz
    plane, y = date // NY, date % NY
    z, xy = plane % nz, (plane // nz) * NY + y
    has_left, has_right = rng > 0, rng < nr - 1
    has_before, has_after = plane > 0, plane < planes - 1

    def z_date(k):
        return ((plane // nz) * nz + (z + k) % nz) * NY + y

    def xy_date(k):
        other = (xy + k) % nxy
        return ((other // NY) * nz + z) * NY + other % NY

    def remote(src, dst, send, recv, to_date, to_rng):
        return pltpu.make_async_remote_copy(
            src_ref=src, dst_ref=dst, send_sem=send, recv_sem=recv,
            device_id=(to_date, to_rng), device_id_type=MESH,
        )

    loads = [
        pltpu.make_async_copy(slc_h.at[0, :, :, pl.ds(128 * p, 128)], samples.at[p], in_sem.at[p])
        for p in range(TILES)
    ]
    for load in loads:
        load.start()
    table_load = pltpu.make_async_copy(table_h, table, in_sem.at[TILES])
    table_load.start()

    barrier = pltpu.get_barrier_semaphore()

    def hello(to_date, to_rng):
        pl.semaphore_signal(barrier, inc=1, device_id=(to_date, to_rng), device_id_type=MESH)

    for k in range(1, nz):
        hello(z_date(k), rng)
    for k in range(1, nxy):
        hello(xy_date(k), rng)
    for present, to_date, to_rng in (
        (has_left, date, rng - 1), (has_right, date, rng + 1),
        (has_before, date - NY, rng), (has_after, date + NY, rng),
    ):
        @pl.when(present)
        def _(to_date=to_date, to_rng=to_rng):
            hello(to_date, to_rng)

    lane = lax.broadcasted_iota(jnp.int32, (LANES, LANES), 1)
    diff = lax.broadcasted_iota(jnp.int32, (LANES, LANES), 0) - lane
    lane8 = lane[0:8]
    rows = tap_rows(off_s, frac_s)
    taps[...] = rows

    @pl.when(jnp.logical_not(has_left))
    def _():
        halo[0] = jnp.zeros((2, ROWS, LANES), BF16)
        tap_halo[0] = jnp.zeros((8, LANES), F32)

    @pl.when(jnp.logical_not(has_right))
    def _():
        halo[1] = jnp.zeros((2, ROWS, LANES), BF16)
        tap_halo[1] = jnp.zeros((8, LANES), F32)

    for h in range(1, SPAN + 1):
        @pl.when(jnp.logical_not(jnp.logical_or(y + h < NY, has_after)))
        def _(h=h):
            coh[h - 1] = jnp.zeros((ROWS, TILES * LANES), BF16)

    root = jnp.where(ref_s[0] == date, 1.0, 0.0).astype(F32)
    for p in range(TILES):
        loads[p].wait()
        real, imag = samples[p, 0].astype(F32), samples[p, 1].astype(F32)
        size = jnp.sqrt(real * real + imag * imag + 1e-06).astype(BF16)
        amp[p] = size
        masked[p] = (size.astype(F32) * root).astype(BF16)

    greeted = (nz - 1) + (nxy - 1)
    for present in (has_left, has_right, has_before, has_after):
        greeted = greeted + present.astype(jnp.int32)
    pl.semaphore_wait(barrier, greeted)

    scatters = []
    for k in range(1, nz):
        to = (z + k) % nz
        scatters.append(
            remote(masked.at[pl.ds(to * ts, ts)], scatter.at[k - 1], rs_send.at[k - 1], rs_recv.at[k - 1],
                   z_date(k), rng)
        )
    to_left = [
        remote(samples.at[0], halo.at[1], halo_send.at[0], halo_recv.at[0], date, rng - 1),
        remote(taps.at[pl.ds(0, 8)], tap_halo.at[1], halo_send.at[1], halo_recv.at[1], date, rng - 1),
    ]
    to_right = [
        remote(samples.at[7], halo.at[0], halo_send.at[2], halo_recv.at[2], date, rng + 1),
        remote(taps.at[pl.ds(8, 8)], tap_halo.at[0], halo_send.at[3], halo_recv.at[3], date, rng + 1),
    ]

    @pl.when(has_left)
    def _():
        for copy in to_left:
            copy.start()

    @pl.when(has_right)
    def _():
        for copy in to_right:
            copy.start()

    for copy in scatters:
        copy.start()

    chunks = ((1, 6), (7, 2), (0, 1))
    nc = len(chunks)

    def item_copies(source, c, slot, send, to_date):
        start, count = chunks[c]
        return remote(
            source.at[pl.ds(start, count)], partner.at[slot, pl.ds(start, count)],
            send, item_recv.at[slot, c], to_date, rng,
        )

    own_dests = [(has_before, SPAN - 1, date - NY)] + [(y >= k, k - 1, date - k) for k in range(1, NY)]
    own_copies = [
        [item_copies(own, c, slot, own_send.at[i, c], to) for c in range(nc)]
        for i, (_, slot, to) in enumerate(own_dests)
    ]
    relay_dests = [
        (jnp.logical_and(has_after, y + k < NY), SPAN - k - 1, date + k) for k in range(1, NY)
    ]
    relay_copies = [
        [item_copies(partner.at[SPAN - 1], c, slot, relay_send.at[i, c], to) for c in range(nc)]
        for i, (_, slot, to) in enumerate(relay_dests)
    ]

    def send_own(c):
        for (present, _, _), copies in zip(own_dests, own_copies):
            @pl.when(present)
            def _(copies=copies):
                copies[c].start()

    def store_own(s, keep=None):
        if s < TILES:
            first, second = rows[2 * s : 2 * s + 1], rows[2 * s + 1 : 2 * s + 2]
        else:
            first, second = tap_halo[1][0:1], tap_halo[0][7:8]
        tile = resample_tile(s, samples, first, second, lane, diff)
        if keep is not None:
            tile = jnp.where(keep, tile, 0.0)
        own[s] = tile.astype(BF16).reshape(2, ROWS, LANES)

    for s in range(1, 7):
        store_own(s)
    send_own(0)

    @pl.when(has_right)
    def _():
        to_left[0].wait_recv()
        to_left[1].wait_recv()

    @pl.when(has_left)
    def _():
        to_right[0].wait_recv()
        to_right[1].wait_recv()

    lane_h = lax.broadcasted_iota(jnp.int32, (2, ROWS, LANES), 2)
    samples[8] = jnp.where(lane_h < 64, halo[1].astype(F32), halo[0].astype(F32)).astype(BF16)
    low_edge = jnp.where(has_right, 64, 0)
    high_edge = jnp.where(has_left, 64, 128)
    store_own(7)
    store_own(8, jnp.logical_or(lane < low_edge, lane >= high_edge))
    send_own(1)
    store_own(0)
    send_own(2)

    for copy in scatters:
        copy.wait_recv()
    total = masked[pl.ds(z * ts, ts)].astype(F32)
    for k in range(nz - 1):
        total = total + scatter[k].astype(F32)
    merged[...] = total.astype(BF16)
    exchanges = [
        remote(merged, exchange.at[k - 1], ae_send.at[k - 1], ae_recv.at[k - 1], xy_date(k), rng)
        for k in range(1, nxy)
    ]
    for copy in exchanges:
        copy.start()

    table_load.wait()
    parts, own_energy = spectrum(amp, table, lane8)
    for p in range(TILES):
        own_spec[p] = parts[p]

    def relay(c):
        @pl.when(has_after)
        def _():
            own_copies[0][c].wait_recv()

        for (present, _, _), copies in zip(relay_dests, relay_copies):
            @pl.when(present)
            def _(copies=copies):
                copies[c].start()

    relay(0)

    for s in range(9):
        real, imag = own[s, 0].astype(F32), own[s, 1].astype(F32)
        fields[s, 0:64] = (real * real + imag * imag).astype(BF16)
    lines = table[LINES : LINES + 192, 0:192]
    for g in range(4):
        box_own[:, 256 * g : 256 * g + 256] = box_group(g, fields, 64, table, table[LINES : LINES + 64, 0:64])

    for copy in exchanges:
        copy.wait_recv()
    total = merged[...].astype(F32)
    for k in range(nxy - 1):
        total = total + exchange[k].astype(F32)
    ref_amp[pl.ds(z * ts, ts)] = total.astype(BF16)
    mine = ref_amp.at[pl.ds(z * ts, ts)]
    gathers = [
        remote(mine, mine, ag_send.at[k - 1], ag_recv.at[k - 1], z_date(k), rng) for k in range(1, nz)
    ]
    for copy in gathers:
        copy.start()

    relay(1)
    relay(2)

    def pair(h):
        slot = h - 1
        if h < SPAN:
            for c in range(nc):
                own_copies[h][c].wait_recv()
        for s in range(9):
            own0, own1 = own[s, 0].astype(F32), own[s, 1].astype(F32)
            other0, other1 = partner[slot, s, 0].astype(F32), partner[slot, s, 1].astype(F32)
            fields[s, 0:64] = (own0 * other0 + own1 * other1).astype(BF16)
            fields[s, 64:128] = (own1 * other0 - own0 * other1).astype(BF16)
            fields[s, 128:192] = (other0 * other0 + other1 * other1).astype(BF16)
        weight = part_s[0, slot].astype(F32)
        for g in range(4):
            box = box_group(g, fields, 192, table, lines)
            re, im, power = box[0:64], box[64:128], box[128:192]
            mine = box_own[:, 256 * g : 256 * g + 256]
            value = weight * (re * re + im * im) / (mine * power + 1e-06)
            coh[slot, :, 256 * g : 256 * g + 256] = value.astype(BF16)

    @pl.when(has_after)
    def _():
        pair(SPAN)

    for h in range(1, NY):
        @pl.when(y + h < NY)
        def _(h=h):
            pair(h)

    for copy in gathers:
        copy.wait_recv()
    ref_parts, ref_energy = spectrum(ref_amp, table, lane8)
    surfaces(own_spec, own_energy, ref_parts, ref_energy, table, surf, lane8)

    for h in range(1, NY):
        @pl.when(y + h >= NY)
        def _(h=h):
            @pl.when(has_after)
            def _():
                pair(h)

    for copy in scatters + exchanges + gathers:
        copy.wait_send()

    @pl.when(has_left)
    def _():
        for copy in to_left:
            copy.wait_send()

    @pl.when(has_right)
    def _():
        for copy in to_right:
            copy.wait_send()

    for dests, copies in ((own_dests, own_copies), (relay_dests, relay_copies)):
        for (present, _, _), mine in zip(dests, copies):
            @pl.when(present)
            def _(mine=mine):
                for copy in mine:
                    copy.wait_send()


def write_kernel(surf, coh, surf_h, coh_h, rows, sem):
    large = pltpu.make_async_copy(coh, coh_h.at[0], sem.at[0])
    large.start()
    for q in range(8):
        rows[:, 128 * q : 128 * q + 128] = surf[:, q, :]
    small = pltpu.make_async_copy(rows, surf_h.at[0, 0], sem.at[1])
    small.start()
    large.wait()
    small.wait()


def body(nz, nx, nr, slc, ref_date, int_offset, frac_offset, partners):
    ts = TILES // nz
    nxy = nx * NY
    smem = pl.BlockSpec(memory_space=pltpu.SMEM)
    anywhere = pl.BlockSpec(memory_space=pl.ANY)
    vmem = pl.BlockSpec(memory_space=pltpu.VMEM)
    dma = pltpu.SemaphoreType.DMA
    tile = (2, ROWS, LANES)
    slab = (TILES, ROWS, LANES)
    surface, coherence = pl.pallas_call(
        functools.partial(kernel, nz, nx, nr),
        out_shape=(
            pltpu.VMEM((16, 8, LANES), F32),
            pltpu.VMEM((SPAN, ROWS, TILES * LANES), BF16),
        ),
        in_specs=[smem, smem, smem, smem, anywhere, anywhere],
        out_specs=(vmem, vmem),
        scratch_shapes=[
            pltpu.VMEM((TABLE_ROWS, 256), BF16),
            pltpu.VMEM((9,) + tile, BF16),
            pltpu.VMEM((2,) + tile, BF16),
            pltpu.VMEM((16, LANES), F32),
            pltpu.VMEM((2, 8, LANES), F32),
            pltpu.VMEM(slab, BF16),
            pltpu.VMEM(slab, BF16),
            pltpu.VMEM((max(nz - 1, 1), ts, ROWS, LANES), BF16),
            pltpu.VMEM((ts, ROWS, LANES), BF16),
            pltpu.VMEM((nxy - 1, ts, ROWS, LANES), BF16),
            pltpu.VMEM(slab, BF16),
            pltpu.VMEM((TILES, 128, LANES), F32),
            pltpu.VMEM((9,) + tile, BF16),
            pltpu.VMEM((SPAN, 9) + tile, BF16),
            pltpu.VMEM((9, 192, LANES), BF16),
            pltpu.VMEM((ROWS, TILES * LANES), F32),
            dma((TILES + 1,)),
            dma((4,)), dma((4,)),
            dma((max(nz - 1, 1),)), dma((max(nz - 1, 1),)),
            dma((nxy - 1,)), dma((nxy - 1,)),
            dma((max(nz - 1, 1),)), dma((max(nz - 1, 1),)),
            dma((4, 3)), dma((3, 3)), dma((4, 3)),
        ],
        compiler_params=pltpu.CompilerParams(collective_id=0, has_side_effects=True),
    )(ref_date, int_offset, frac_offset, partners, slc, tables())
    return pl.pallas_call(
        write_kernel,
        out_shape=(
            jax.ShapeDtypeStruct((1, 1, 16, 1024), F32),
            jax.ShapeDtypeStruct((1, SPAN, ROWS, TILES * LANES), BF16),
        ),
        in_specs=[vmem, vmem],
        out_specs=(anywhere, anywhere),
        scratch_shapes=[pltpu.VMEM((16, 1024), F32), dma((2,))],
    )(*(pltpu.with_memory_space_constraint(x, pltpu.VMEM) for x in (surface, coherence)))


def solution(mesh):
    dates, nr = mesh.shape["date"], mesh.shape["rng"]
    planes = dates // NY
    nz = min(planes, 8)
    in_specs = (
        P("date", None, None, "rng"),
        P(),
        P("date", None, "rng"),
        P("date", None, "rng"),
        P("date", None),
    )
    out_specs = (P("date", None, "rng", None), P("date", None, None, "rng"))
    return jax.shard_map(
        functools.partial(body, nz, planes // nz, nr),
        mesh=mesh, in_specs=in_specs, out_specs=out_specs, check_vma=False,
    )
```

```python
import functools

import jax
import jax.numpy as jnp
import numpy as np
from jax import lax
from jax.experimental import pallas as pl
from jax.experimental.pallas import tpu as pltpu
from jax.sharding import PartitionSpec as P

BLK = 64
LAGS = 32
SPAN = 4
NY = 4
TILES = 8
ROWS = 64
LANES = 128
MESH = pl.DeviceIdType.MESH
F32 = jnp.float32
BF16 = jnp.bfloat16

RIGHT, LEFT, VRIGHT, VLEFT, COLS, LINES, TABLE_ROWS = 0, 128, 256, 512, 544, 1056, 1248


def tables():
    n = np.arange(BLK)
    angle = 2.0 * np.pi / BLK * (n[:, None] * n[None, :] % BLK)
    cosine, sine = np.cos(angle), np.sin(angle)
    signed = np.where(n < BLK // 2, n, n - BLK)
    lag = np.arange(LAGS) - LAGS // 2
    lag_angle = 2.0 * np.pi / (2 * BLK) * (lag[:, None] * signed[None, :] % (2 * BLK))
    lag_cos, lag_sin = np.cos(lag_angle), np.sin(lag_angle)
    table = np.zeros((TABLE_ROWS, 256), np.float64)
    for b in range(2):
        rows = slice(RIGHT + 64 * b, RIGHT + 64 * b + 64)
        table[rows, 64 * b : 64 * b + 64] = cosine
        table[rows, 128 + 64 * b : 128 + 64 * b + 64] = sine
        rows = slice(VRIGHT + 64 * b, VRIGHT + 64 * b + 64)
        table[rows, 128 * b : 128 * b + 128] = np.tile(lag_cos.T, (1, 4))
        rows = slice(VRIGHT + 128 + 64 * b, VRIGHT + 128 + 64 * b + 64)
        table[rows, 128 * b : 128 * b + 128] = np.tile(lag_sin.T, (1, 4))
    table[LEFT : LEFT + 64, 0:64] = cosine
    table[LEFT : LEFT + 64, 64:128] = -sine
    table[LEFT + 64 : LEFT + 128, 0:64] = -sine
    table[LEFT + 64 : LEFT + 128, 64:128] = -cosine
    order = np.array([4 * q + i for i in range(4) for q in range(8)])
    table[VLEFT : VLEFT + 32] = np.concatenate([lag_cos, -lag_sin, -lag_sin, -lag_cos], axis=1)[order]
    c, r = np.arange(512)[:, None], np.arange(256)[None, :]
    table[COLS : COLS + 512] = np.abs(c - 128 - r) <= 9
    c, r = np.arange(192)[:, None], np.arange(192)[None, :]
    table[LINES : LINES + 192, 0:192] = (np.abs(c - r) <= 2) & (c // 64 == r // 64)
    return jnp.asarray(table, BF16)


def tap_rows(off_s, frac_s):
    row = lax.broadcasted_iota(jnp.int32, (16, LANES), 0)
    lane = lax.broadcasted_iota(jnp.int32, (16, LANES), 1)
    off = jnp.zeros((16, LANES), jnp.int32)
    frac = jnp.zeros((16, LANES), F32)
    for j in range(16):
        off = jnp.where(row == j, off_s[0, 0, j], off)
        frac = jnp.where(row == j, frac_s[0, 0, j], frac)
    u = jnp.where(lane < 64, -lane, 128 - lane) - off
    valid = (u >= -3) & (u <= 4)
    uf = u.astype(F32)
    x = uf - frac
    near = jnp.minimum(frac, 1.0 - frac)
    a = near * np.float32(np.pi)
    a2 = a * a
    series = np.float32(1.6059044e-10)
    for coefficient in (-2.5052108e-8, 2.7557319e-6, -1.9841270e-4, 8.3333333e-3, -1.6666667e-1, 1.0):
        series = series * a2 + np.float32(coefficient)
    sine = a * series
    sign = jnp.where((u & 1) == 0, -1.0, 1.0)
    zero = x == 0.0
    sinc = jnp.where(zero, 1.0, sign * sine / jnp.where(zero, 1.0, np.float32(np.pi) * x))
    b = x * np.float32(np.pi / 8)
    b2 = b * b
    half = np.float32(-1.1470746e-11)
    for coefficient in (2.0876757e-9, -2.7557319e-7, 2.4801587e-5, -1.3888889e-3, 4.1666667e-2, -0.5, 1.0):
        half = half * b2 + np.float32(coefficient)
    return jnp.where(valid, sinc * half * half, 0.0)


def resample_tile(s, samples, first, second, lane, diff):
    first = jnp.broadcast_to(first, (LANES, LANES))
    second = jnp.broadcast_to(second, (LANES, LANES))
    first = pltpu.roll(first, 0, 1, stride=1, stride_axis=0)
    second = pltpu.roll(second, 0, 1, stride=1, stride_axis=0)
    band = jnp.where(lane < 64, first, second)
    high = band.astype(BF16).astype(F32)
    low = band - high
    parts = []
    for keep in (diff >= 64, jnp.abs(diff) < 64, diff <= -64):
        parts.append(
            jnp.concatenate(
                [jnp.where(keep, high, 0.0).astype(BF16), jnp.where(keep, low, 0.0).astype(BF16)], axis=1
            )
        )
    weights = jnp.concatenate(parts, axis=0)
    window = jnp.concatenate(
        [samples[i].reshape(128, LANES) for i in ((s + 8) % 9, s, (s + 1) % 9)], axis=1
    )
    both = jnp.dot(window, weights, preferred_element_type=F32)
    return both[:, 0:LANES] + both[:, LANES:256]


def halves(rows, lane):
    left = jnp.sum(jnp.where(lane < 64, rows, 0.0), axis=1, keepdims=True)
    right = jnp.sum(jnp.where(lane < 64, 0.0, rows), axis=1, keepdims=True)
    return jnp.where(lane < 64, left, right)


def spectrum(amp, table, lane8):
    blocks = [amp[p].astype(F32) for p in range(TILES)]
    sums = jnp.concatenate([jnp.sum(b, axis=0, keepdims=True) for b in blocks], axis=0)
    mean = halves(sums, lane8) * np.float32(1.0 / (BLK * BLK))
    centered = [b - mean[p : p + 1] for p, b in enumerate(blocks)]
    squares = jnp.concatenate([jnp.sum(c * c, axis=0, keepdims=True) for c in centered], axis=0)
    energy = halves(squares, lane8)
    stacked = jnp.concatenate([c.astype(BF16) for c in centered], axis=0)
    along = jnp.dot(stacked, table[RIGHT : RIGHT + 128, :], preferred_element_type=F32)
    parts = []
    for p in range(TILES):
        part = along[64 * p : 64 * p + 64]
        parts.append(jnp.concatenate([part[:, 0:128], part[:, 128:256]], axis=0).astype(BF16))
    full = jnp.dot(
        table[LEFT : LEFT + 128, 0:128], jnp.concatenate(parts, axis=1), preferred_element_type=F32
    )
    return [full[:, 128 * p : 128 * p + 128] for p in range(TILES)], energy


def surfaces(own_spec, own_energy, ref_parts, ref_energy, table, out, lane8):
    scale = 1.0 / (np.float32(BLK) * jnp.sqrt(own_energy * ref_energy + 1e-06))
    vleft = table[VLEFT : VLEFT + 32, :]
    crosses = []
    for p in range(TILES):
        own_real, own_imag = own_spec[p, 0:64], own_spec[p, 64:128]
        ref_real, ref_imag = ref_parts[p][0:64], ref_parts[p][64:128]
        crosses.append((own_real * ref_real + own_imag * ref_imag).astype(BF16))
        crosses.append((own_imag * ref_real - own_real * ref_imag).astype(BF16))
    crosses = jnp.concatenate(crosses, axis=0)
    cos_part, sin_part = (
        jnp.dot(crosses, table[top : top + 128, :], preferred_element_type=F32).astype(BF16)
        for top in (VRIGHT, VRIGHT + 128)
    )
    for p in range(TILES):
        rows = slice(128 * p, 128 * p + 128)
        turned = jnp.concatenate([cos_part[rows], sin_part[rows]], axis=0)
        value = jnp.dot(vleft, turned, preferred_element_type=F32)
        for b in range(2):
            half = value[:, 128 * b : 128 * b + 128]
            picked = half[0:8]
            for i in range(1, 4):
                picked = jnp.where(lane8 >= 32 * i, half[8 * i : 8 * i + 8], picked)
            out[2 * p + b] = picked * jnp.broadcast_to(scale[p : p + 1, 64 * b : 64 * b + 1], (8, LANES))


def at(s):
    return (s + 1) % TILES if s < TILES else TILES


def pack_edge(tile, lane):
    turned = pltpu.roll(tile, 16, 1)
    packed = turned[0:32]
    for k in range(1, 4):
        packed = jnp.where(lane[0:32] >= 32 * k, pltpu.roll(turned[32 * k : 32 * k + 32], 32 * k, 1), packed)
    return packed


def unpack_edge(packed, lane):
    keep = jnp.logical_or(lane[0:32] < 16, lane[0:32] >= 112)
    parts = [jnp.where(keep, pltpu.roll(packed, 112 - 32 * k, 1), 0.0) for k in range(4)]
    return jnp.concatenate(parts, axis=0)


def boxes(fields, rows, table):
    windows = [
        jnp.concatenate([fields[i, 0:rows] for i in ((2 * g + 8) % 9, 2 * g, 2 * g + 1, 2 * g + 2)], axis=1)
        for g in range(4)
    ]
    summed = jnp.dot(
        jnp.concatenate(windows, axis=0), table[COLS : COLS + 512, :], preferred_element_type=F32
    ).astype(BF16)
    summed = jnp.concatenate([summed[rows * g : rows * g + rows] for g in range(4)], axis=1)
    return jnp.dot(table[LINES : LINES + rows, 0:rows], summed, preferred_element_type=F32)


def kernel(
    nz, nx, nr,
    ref_s, off_s, frac_s, part_s, slc_h, table_h,
    surf, coh,
    table, samples, halo, taps, tap_halo, amp, masked, scatter, merged, exchange, ref_amp,
    own_spec, own, edge, partner, partner_edge, fields, box_own,
    in_sem, halo_send, halo_recv, rs_send, rs_recv, ae_send, ae_recv, ag_send, ag_recv,
    own_send, relay_send, item_recv,
):
    date, rng = lax.axis_index("date"), lax.axis_index("rng")
    planes = nx * nz
    nxy = nx * NY
    ts = TILES // nz
    plane, y = date // NY, date % NY
    z, xy = plane % nz, (plane // nz) * NY + y
    has_left, has_right = rng > 0, rng < nr - 1
    has_before, has_after = plane > 0, plane < planes - 1

    def z_date(k):
        return ((plane // nz) * nz + (z + k) % nz) * NY + y

    def xy_date(k):
        other = (xy + k) % nxy
        return ((other // NY) * nz + z) * NY + other % NY

    def remote(src, dst, send, recv, to_date, to_rng):
        return pltpu.make_async_remote_copy(
            src_ref=src, dst_ref=dst, send_sem=send, recv_sem=recv,
            device_id=(to_date, to_rng), device_id_type=MESH,
        )

    loads = [
        pltpu.make_async_copy(slc_h.at[0, :, :, pl.ds(128 * p, 128)], samples.at[p], in_sem.at[p])
        for p in range(TILES)
    ]
    for load in loads:
        load.start()
    table_load = pltpu.make_async_copy(table_h, table, in_sem.at[TILES])
    table_load.start()

    barrier = pltpu.get_barrier_semaphore()

    def hello(to_date, to_rng):
        pl.semaphore_signal(barrier, inc=1, device_id=(to_date, to_rng), device_id_type=MESH)

    for k in range(1, nz):
        hello(z_date(k), rng)
    for k in range(1, nxy):
        hello(xy_date(k), rng)
    for present, to_date, to_rng in (
        (has_left, date, rng - 1), (has_right, date, rng + 1),
        (has_before, date - NY, rng), (has_after, date + NY, rng),
    ):
        @pl.when(present)
        def _(to_date=to_date, to_rng=to_rng):
            hello(to_date, to_rng)

    lane = lax.broadcasted_iota(jnp.int32, (LANES, LANES), 1)
    diff = lax.broadcasted_iota(jnp.int32, (LANES, LANES), 0) - lane
    lane8 = lane[0:8]
    rows = tap_rows(off_s, frac_s)
    taps[...] = rows

    @pl.when(jnp.logical_not(has_left))
    def _():
        halo[0] = jnp.zeros((2, ROWS, LANES), BF16)
        tap_halo[0] = jnp.zeros((8, LANES), F32)

    @pl.when(jnp.logical_not(has_right))
    def _():
        halo[1] = jnp.zeros((2, ROWS, LANES), BF16)
        tap_halo[1] = jnp.zeros((8, LANES), F32)

    for h in range(1, SPAN + 1):
        @pl.when(jnp.logical_not(jnp.logical_or(y + h < NY, has_after)))
        def _(h=h):
            coh[h - 1] = jnp.zeros((ROWS, TILES * LANES), BF16)

    root = jnp.where(ref_s[0] == date, 1.0, 0.0).astype(F32)
    for p in range(TILES):
        loads[p].wait()
        real, imag = samples[p, 0].astype(F32), samples[p, 1].astype(F32)
        size = jnp.sqrt(real * real + imag * imag + 1e-06).astype(BF16)
        amp[p] = size
        masked[p] = (size.astype(F32) * root).astype(BF16)

    greeted = (nz - 1) + (nxy - 1)
    for present in (has_left, has_right, has_before, has_after):
        greeted = greeted + present.astype(jnp.int32)
    pl.semaphore_wait(barrier, greeted)

    scatters = []
    for k in range(1, nz):
        to = (z + k) % nz
        scatters.append(
            remote(masked.at[pl.ds(to * ts, ts)], scatter.at[k - 1], rs_send.at[k - 1], rs_recv.at[k - 1],
                   z_date(k), rng)
        )
    to_left = [
        remote(samples.at[0], halo.at[1], halo_send.at[0], halo_recv.at[0], date, rng - 1),
        remote(taps.at[pl.ds(0, 8)], tap_halo.at[1], halo_send.at[1], halo_recv.at[1], date, rng - 1),
    ]
    to_right = [
        remote(samples.at[7], halo.at[0], halo_send.at[2], halo_recv.at[2], date, rng + 1),
        remote(taps.at[pl.ds(8, 8)], tap_halo.at[0], halo_send.at[3], halo_recv.at[3], date, rng + 1),
    ]

    @pl.when(has_left)
    def _():
        for copy in to_left:
            copy.start()

    @pl.when(has_right)
    def _():
        for copy in to_right:
            copy.start()

    for copy in scatters:
        copy.start()

    chunks = ((2, 6), (0, 2))
    nc = len(chunks) + 1

    def item_copies(source, source_edge, slot, sends, to_date):
        copies = [
            remote(
                source.at[pl.ds(start, count)], partner.at[slot, pl.ds(start, count)],
                sends.at[c], item_recv.at[slot, c], to_date, rng,
            )
            for c, (start, count) in enumerate(chunks)
        ]
        copies.append(
            remote(source_edge, partner_edge.at[slot], sends.at[nc - 1], item_recv.at[slot, nc - 1], to_date, rng)
        )
        return copies

    own_dests = [(has_before, 3, date - NY), (y >= 1, 0, date - 1), (y >= 3, 2, date - 3)]
    own_copies = [item_copies(own, edge, slot, own_send.at[i], to) for i, (_, slot, to) in enumerate(own_dests)]
    middle = jnp.logical_and(y >= 1, y + 1 < NY)
    relay_dests = [
        (jnp.logical_and(has_after, y + 1 < NY), 3, 2, date + 1),
        (jnp.logical_and(has_after, y + 3 < NY), 3, 0, date + 3),
        (middle, 0, 1, date - 1),
        (jnp.logical_and(has_after, middle), 2, 1, date + 1),
    ]
    relay_copies = [
        item_copies(partner.at[source], partner_edge.at[source], slot, relay_send.at[i], to)
        for i, (_, source, slot, to) in enumerate(relay_dests)
    ]

    def arrived(slot, c):
        remote(
            edge if c == nc - 1 else own.at[pl.ds(*chunks[c])],
            partner_edge.at[slot] if c == nc - 1 else partner.at[slot, pl.ds(*chunks[c])],
            own_send.at[0, c], item_recv.at[slot, c], date, rng,
        ).wait_recv()

    def send_own(c, which):
        for i in which:
            @pl.when(own_dests[i][0])
            def _(i=i):
                own_copies[i][c].start()

    def store_own(s, keep=None):
        if s < TILES:
            first, second = rows[2 * s : 2 * s + 1], rows[2 * s + 1 : 2 * s + 2]
        else:
            first, second = tap_halo[1][0:1], tap_halo[0][7:8]
        tile = resample_tile(s, samples, first, second, lane, diff)
        if keep is not None:
            tile = jnp.where(keep, tile, 0.0)
            edge[...] = pack_edge(tile, lane).astype(BF16)
        own[at(s)] = tile.astype(BF16).reshape(2, ROWS, LANES)

    for s in range(1, 7):
        store_own(s)
    send_own(0, (0, 1, 2))

    @pl.when(has_right)
    def _():
        to_left[0].wait_recv()
        to_left[1].wait_recv()

    @pl.when(has_left)
    def _():
        to_right[0].wait_recv()
        to_right[1].wait_recv()

    lane_h = lax.broadcasted_iota(jnp.int32, (2, ROWS, LANES), 2)
    samples[8] = jnp.where(lane_h < 64, halo[1].astype(F32), halo[0].astype(F32)).astype(BF16)
    low_edge = jnp.where(has_right, 64, 0)
    high_edge = jnp.where(has_left, 64, 128)
    store_own(7)
    store_own(8, jnp.logical_or(lane < low_edge, lane >= high_edge))
    store_own(0)
    send_own(1, (0, 1, 2))
    send_own(2, (0, 1, 2))

    for copy in scatters:
        copy.wait_recv()
    total = masked[pl.ds(z * ts, ts)].astype(F32)
    for k in range(nz - 1):
        total = total + scatter[k].astype(F32)
    merged[...] = total.astype(BF16)
    exchanges = [
        remote(merged, exchange.at[k - 1], ae_send.at[k - 1], ae_recv.at[k - 1], xy_date(k), rng)
        for k in range(1, nxy)
    ]
    for copy in exchanges:
        copy.start()

    table_load.wait()
    parts, own_energy = spectrum(amp, table, lane8)
    for p in range(TILES):
        own_spec[p] = parts[p]

    def relay(source, c):
        exists = {0: y + 1 < NY, 2: jnp.logical_and(has_after, y >= 1), 3: has_after}[source]

        @pl.when(exists)
        def _():
            arrived(source, c)

        for (present, at_slot, _, _), copies in zip(relay_dests, relay_copies):
            if at_slot == source:
                @pl.when(present)
                def _(copies=copies):
                    copies[c].start()

    relay(0, 0)
    relay(3, 0)

    for s in range(9):
        real, imag = own[at(s), 0].astype(F32), own[at(s), 1].astype(F32)
        fields[s, 0:64] = (real * real + imag * imag).astype(BF16)
    box_own[...] = boxes(fields, 64, table)

    for copy in exchanges:
        copy.wait_recv()
    total = merged[...].astype(F32)
    for k in range(nxy - 1):
        total = total + exchange[k].astype(F32)
    ref_amp[pl.ds(z * ts, ts)] = total.astype(BF16)
    mine = ref_amp.at[pl.ds(z * ts, ts)]
    gathers = [
        remote(mine, mine, ag_send.at[k - 1], ag_recv.at[k - 1], z_date(k), rng) for k in range(1, nz)
    ]
    for copy in gathers:
        copy.start()

    for c in range(1, nc):
        relay(0, c)
        relay(3, c)

    def pair(h):
        slot = h - 1
        partner[slot, TILES] = unpack_edge(partner_edge[slot].astype(F32), lane).astype(BF16).reshape(2, ROWS, LANES)
        for s in range(9):
            own0, own1 = own[at(s), 0].astype(F32), own[at(s), 1].astype(F32)
            other0, other1 = partner[slot, at(s), 0].astype(F32), partner[slot, at(s), 1].astype(F32)
            fields[s, 0:64] = (own0 * other0 + own1 * other1).astype(BF16)
            fields[s, 64:128] = (own1 * other0 - own0 * other1).astype(BF16)
            fields[s, 128:192] = (other0 * other0 + other1 * other1).astype(BF16)
        weight = part_s[0, slot].astype(F32)
        box = boxes(fields, 192, table)
        re, im, power = box[0:64], box[64:128], box[128:192]
        coh[slot] = (weight * (re * re + im * im) / (box_own[...] * power + 1e-06)).astype(BF16)

    @pl.when(has_after)
    def _():
        pair(SPAN)

    @pl.when(y + 1 < NY)
    def _():
        pair(1)

    for c in range(nc):
        relay(2, c)

    @pl.when(y + 3 < NY)
    def _():
        for c in range(nc):
            arrived(2, c)
        pair(3)

    @pl.when(jnp.logical_and(has_after, y >= 1))
    def _():
        pair(3)

    for copy in gathers:
        copy.wait_recv()
    ref_parts, ref_energy = spectrum(ref_amp, table, lane8)
    surfaces(own_spec, own_energy, ref_parts, ref_energy, table, surf, lane8)

    @pl.when(jnp.logical_or(y + 2 < NY, has_after))
    def _():
        for c in range(nc):
            arrived(1, c)
        pair(2)

    @pl.when(jnp.logical_and(has_after, y + 1 >= NY))
    def _():
        for c in range(nc):
            arrived(0, c)
        pair(1)

    for copy in scatters + exchanges + gathers:
        copy.wait_send()

    @pl.when(has_left)
    def _():
        for copy in to_left:
            copy.wait_send()

    @pl.when(has_right)
    def _():
        for copy in to_right:
            copy.wait_send()

    for dests, copies in ((own_dests, own_copies), (relay_dests, relay_copies)):
        for (present, *_), mine in zip(dests, copies):
            @pl.when(present)
            def _(mine=mine):
                for copy in mine:
                    copy.wait_send()


def write_kernel(surf, coh, surf_h, coh_h, rows, sem):
    large = pltpu.make_async_copy(coh, coh_h.at[0], sem.at[0])
    large.start()
    for q in range(8):
        rows[:, 128 * q : 128 * q + 128] = surf[:, q, :]
    small = pltpu.make_async_copy(rows, surf_h.at[0, 0], sem.at[1])
    small.start()
    large.wait()
    small.wait()


def body(nz, nx, nr, slc, ref_date, int_offset, frac_offset, partners):
    ts = TILES // nz
    nxy = nx * NY
    smem = pl.BlockSpec(memory_space=pltpu.SMEM)
    anywhere = pl.BlockSpec(memory_space=pl.ANY)
    vmem = pl.BlockSpec(memory_space=pltpu.VMEM)
    dma = pltpu.SemaphoreType.DMA
    tile = (2, ROWS, LANES)
    slab = (TILES, ROWS, LANES)
    surface, coherence = pl.pallas_call(
        functools.partial(kernel, nz, nx, nr),
        out_shape=(
            pltpu.VMEM((16, 8, LANES), F32),
            pltpu.VMEM((SPAN, ROWS, TILES * LANES), BF16),
        ),
        in_specs=[smem, smem, smem, smem, anywhere, anywhere],
        out_specs=(vmem, vmem),
        scratch_shapes=[
            pltpu.VMEM((TABLE_ROWS, 256), BF16),
            pltpu.VMEM((9,) + tile, BF16),
            pltpu.VMEM((2,) + tile, BF16),
            pltpu.VMEM((16, LANES), F32),
            pltpu.VMEM((2, 8, LANES), F32),
            pltpu.VMEM(slab, BF16),
            pltpu.VMEM(slab, BF16),
            pltpu.VMEM((max(nz - 1, 1), ts, ROWS, LANES), BF16),
            pltpu.VMEM((ts, ROWS, LANES), BF16),
            pltpu.VMEM((nxy - 1, ts, ROWS, LANES), BF16),
            pltpu.VMEM(slab, BF16),
            pltpu.VMEM((TILES, 128, LANES), F32),
            pltpu.VMEM((9,) + tile, BF16),
            pltpu.VMEM((32, LANES), BF16),
            pltpu.VMEM((SPAN, 9) + tile, BF16),
            pltpu.VMEM((SPAN, 32, LANES), BF16),
            pltpu.VMEM((9, 192, LANES), BF16),
            pltpu.VMEM((ROWS, TILES * LANES), F32),
            dma((TILES + 1,)),
            dma((4,)), dma((4,)),
            dma((max(nz - 1, 1),)), dma((max(nz - 1, 1),)),
            dma((nxy - 1,)), dma((nxy - 1,)),
            dma((max(nz - 1, 1),)), dma((max(nz - 1, 1),)),
            dma((3, 3)), dma((4, 3)), dma((4, 3)),
        ],
        compiler_params=pltpu.CompilerParams(collective_id=0, has_side_effects=True),
    )(ref_date, int_offset, frac_offset, partners, slc, tables())
    return pl.pallas_call(
        write_kernel,
        out_shape=(
            jax.ShapeDtypeStruct((1, 1, 16, 1024), F32),
            jax.ShapeDtypeStruct((1, SPAN, ROWS, TILES * LANES), BF16),
        ),
        in_specs=[vmem, vmem],
        out_specs=(anywhere, anywhere),
        scratch_shapes=[pltpu.VMEM((16, 1024), F32), dma((2,))],
    )(*(pltpu.with_memory_space_constraint(x, pltpu.VMEM) for x in (surface, coherence)))


def solution(mesh):
    dates, nr = mesh.shape["date"], mesh.shape["rng"]
    planes = dates // NY
    nz = min(planes, 8)
    in_specs = (
        P("date", None, None, "rng"),
        P(),
        P("date", None, "rng"),
        P("date", None, "rng"),
        P("date", None),
    )
    out_specs = (P("date", None, "rng", None), P("date", None, None, "rng"))
    return jax.shard_map(
        functools.partial(body, nz, planes // nz, nr),
        mesh=mesh, in_specs=in_specs, out_specs=out_specs, check_vma=False,
    )
```

```python
import functools

import jax
import jax.numpy as jnp
import numpy as np
from jax import lax
from jax.experimental import pallas as pl
from jax.experimental.pallas import tpu as pltpu
from jax.sharding import PartitionSpec as P

BLK = 64
LAGS = 32
SPAN = 4
NY = 4
TILES = 8
ROWS = 64
LANES = 128
MESH = pl.DeviceIdType.MESH
F32 = jnp.float32
BF16 = jnp.bfloat16

RIGHT, LEFT, VRIGHT, VLEFT, COLS, LINES, TABLE_ROWS = 0, 128, 256, 512, 544, 1056, 1248


def tables():
    n = np.arange(BLK)
    angle = 2.0 * np.pi / BLK * (n[:, None] * n[None, :] % BLK)
    cosine, sine = np.cos(angle), np.sin(angle)
    signed = np.where(n < BLK // 2, n, n - BLK)
    lag = np.arange(LAGS) - LAGS // 2
    lag_angle = 2.0 * np.pi / (2 * BLK) * (lag[:, None] * signed[None, :] % (2 * BLK))
    lag_cos, lag_sin = np.cos(lag_angle), np.sin(lag_angle)
    table = np.zeros((TABLE_ROWS, 256), np.float64)
    for b in range(2):
        rows = slice(RIGHT + 64 * b, RIGHT + 64 * b + 64)
        table[rows, 64 * b : 64 * b + 64] = cosine
        table[rows, 128 + 64 * b : 128 + 64 * b + 64] = sine
        rows = slice(VRIGHT + 64 * b, VRIGHT + 64 * b + 64)
        table[rows, 128 * b : 128 * b + 128] = np.tile(lag_cos.T, (1, 4))
        rows = slice(VRIGHT + 128 + 64 * b, VRIGHT + 128 + 64 * b + 64)
        table[rows, 128 * b : 128 * b + 128] = np.tile(lag_sin.T, (1, 4))
    table[LEFT : LEFT + 64, 0:64] = cosine
    table[LEFT : LEFT + 64, 64:128] = -sine
    table[LEFT + 64 : LEFT + 128, 0:64] = -sine
    table[LEFT + 64 : LEFT + 128, 64:128] = -cosine
    order = np.array([4 * q + i for i in range(4) for q in range(8)])
    table[VLEFT : VLEFT + 32] = np.concatenate([lag_cos, -lag_sin, -lag_sin, -lag_cos], axis=1)[order]
    c, r = np.arange(512)[:, None], np.arange(256)[None, :]
    table[COLS : COLS + 512] = np.abs(c - 128 - r) <= 9
    c, r = np.arange(192)[:, None], np.arange(192)[None, :]
    table[LINES : LINES + 192, 0:192] = (np.abs(c - r) <= 2) & (c // 64 == r // 64)
    return jnp.asarray(table, BF16)


def tap_rows(off_s, frac_s):
    row = lax.broadcasted_iota(jnp.int32, (16, LANES), 0)
    lane = lax.broadcasted_iota(jnp.int32, (16, LANES), 1)
    off = jnp.zeros((16, LANES), jnp.int32)
    frac = jnp.zeros((16, LANES), F32)
    for j in range(16):
        off = jnp.where(row == j, off_s[0, 0, j], off)
        frac = jnp.where(row == j, frac_s[0, 0, j], frac)
    u = jnp.where(lane < 64, -lane, 128 - lane) - off
    valid = (u >= -3) & (u <= 4)
    uf = u.astype(F32)
    x = uf - frac
    near = jnp.minimum(frac, 1.0 - frac)
    a = near * np.float32(np.pi)
    a2 = a * a
    series = np.float32(1.6059044e-10)
    for coefficient in (-2.5052108e-8, 2.7557319e-6, -1.9841270e-4, 8.3333333e-3, -1.6666667e-1, 1.0):
        series = series * a2 + np.float32(coefficient)
    sine = a * series
    sign = jnp.where((u & 1) == 0, -1.0, 1.0)
    zero = x == 0.0
    sinc = jnp.where(zero, 1.0, sign * sine / jnp.where(zero, 1.0, np.float32(np.pi) * x))
    b = x * np.float32(np.pi / 8)
    b2 = b * b
    half = np.float32(-1.1470746e-11)
    for coefficient in (2.0876757e-9, -2.7557319e-7, 2.4801587e-5, -1.3888889e-3, 4.1666667e-2, -0.5, 1.0):
        half = half * b2 + np.float32(coefficient)
    return jnp.where(valid, sinc * half * half, 0.0)


def resample_tile(s, samples, first, second, lane, diff):
    first = jnp.broadcast_to(first, (LANES, LANES))
    second = jnp.broadcast_to(second, (LANES, LANES))
    first = pltpu.roll(first, 0, 1, stride=1, stride_axis=0)
    second = pltpu.roll(second, 0, 1, stride=1, stride_axis=0)
    band = jnp.where(lane < 64, first, second)
    high = band.astype(BF16).astype(F32)
    low = band - high
    parts = []
    for keep in (diff >= 64, jnp.abs(diff) < 64, diff <= -64):
        parts.append(
            jnp.concatenate(
                [jnp.where(keep, high, 0.0).astype(BF16), jnp.where(keep, low, 0.0).astype(BF16)], axis=1
            )
        )
    weights = jnp.concatenate(parts, axis=0)
    window = jnp.concatenate(
        [samples[i].reshape(128, LANES) for i in ((s + 8) % 9, s, (s + 1) % 9)], axis=1
    )
    both = jnp.dot(window, weights, preferred_element_type=F32)
    return both[:, 0:LANES] + both[:, LANES:256]


def halves(rows, lane):
    left = jnp.sum(jnp.where(lane < 64, rows, 0.0), axis=1, keepdims=True)
    right = jnp.sum(jnp.where(lane < 64, 0.0, rows), axis=1, keepdims=True)
    return jnp.where(lane < 64, left, right)


def spectrum(amp, table, lane8):
    blocks = [amp[p].astype(F32) for p in range(TILES)]
    sums = jnp.concatenate([jnp.sum(b, axis=0, keepdims=True) for b in blocks], axis=0)
    mean = halves(sums, lane8) * np.float32(1.0 / (BLK * BLK))
    centered = [b - mean[p : p + 1] for p, b in enumerate(blocks)]
    squares = jnp.concatenate([jnp.sum(c * c, axis=0, keepdims=True) for c in centered], axis=0)
    energy = halves(squares, lane8)
    stacked = jnp.concatenate([c.astype(BF16) for c in centered], axis=0)
    along = jnp.dot(stacked, table[RIGHT : RIGHT + 128, :], preferred_element_type=F32)
    parts = []
    for p in range(TILES):
        part = along[64 * p : 64 * p + 64]
        parts.append(jnp.concatenate([part[:, 0:128], part[:, 128:256]], axis=0).astype(BF16))
    full = jnp.dot(
        table[LEFT : LEFT + 128, 0:128], jnp.concatenate(parts, axis=1), preferred_element_type=F32
    )
    return [full[:, 128 * p : 128 * p + 128] for p in range(TILES)], energy


def surfaces(own_spec, own_energy, ref_parts, ref_energy, table, out, lane8):
    scale = 1.0 / (np.float32(BLK) * jnp.sqrt(own_energy * ref_energy + 1e-06))
    vleft = table[VLEFT : VLEFT + 32, :]
    crosses = []
    for p in range(TILES):
        own_real, own_imag = own_spec[p, 0:64], own_spec[p, 64:128]
        ref_real, ref_imag = ref_parts[p][0:64], ref_parts[p][64:128]
        crosses.append((own_real * ref_real + own_imag * ref_imag).astype(BF16))
        crosses.append((own_imag * ref_real - own_real * ref_imag).astype(BF16))
    crosses = jnp.concatenate(crosses, axis=0)
    cos_part, sin_part = (
        jnp.dot(crosses, table[top : top + 128, :], preferred_element_type=F32).astype(BF16)
        for top in (VRIGHT, VRIGHT + 128)
    )
    for p in range(TILES):
        rows = slice(128 * p, 128 * p + 128)
        turned = jnp.concatenate([cos_part[rows], sin_part[rows]], axis=0)
        value = jnp.dot(vleft, turned, preferred_element_type=F32)
        for b in range(2):
            half = value[:, 128 * b : 128 * b + 128]
            picked = half[0:8]
            for i in range(1, 4):
                picked = jnp.where(lane8 >= 32 * i, half[8 * i : 8 * i + 8], picked)
            out[2 * p + b] = picked * jnp.broadcast_to(scale[p : p + 1, 64 * b : 64 * b + 1], (8, LANES))


def at(s):
    return (s + 1) % TILES if s < TILES else TILES


def pack_edge(tile, lane):
    turned = pltpu.roll(tile, 16, 1)
    packed = turned[0:32]
    for k in range(1, 4):
        packed = jnp.where(lane[0:32] >= 32 * k, pltpu.roll(turned[32 * k : 32 * k + 32], 32 * k, 1), packed)
    return packed


def unpack_edge(packed, lane):
    keep = jnp.logical_or(lane[0:32] < 16, lane[0:32] >= 112)
    parts = [jnp.where(keep, pltpu.roll(packed, 112 - 32 * k, 1), 0.0) for k in range(4)]
    return jnp.concatenate(parts, axis=0)


def boxes(fields, rows, table):
    windows = [
        jnp.concatenate([fields[i, 0:rows] for i in ((2 * g + 8) % 9, 2 * g, 2 * g + 1, 2 * g + 2)], axis=1)
        for g in range(4)
    ]
    summed = jnp.dot(
        jnp.concatenate(windows, axis=0), table[COLS : COLS + 512, :], preferred_element_type=F32
    ).astype(BF16)
    summed = jnp.concatenate([summed[rows * g : rows * g + rows] for g in range(4)], axis=1)
    return jnp.dot(table[LINES : LINES + rows, 0:rows], summed, preferred_element_type=F32)


def kernel(
    nz, nx, nr,
    ref_h, off_h, frac_h, part_h, slc_h, table_h,
    surf, coh,
    table, samples, halo, taps, tap_halo, amp, masked, scatter, merged, exchange, ref_amp,
    own_spec, own, edge, partner, partner_edge, fields, box_own,
    in_sem, halo_send, halo_recv, rs_send, rs_recv, ae_send, ae_recv, ag_send, ag_recv,
    own_send, relay_send, item_recv, scalar_sem, ref_s, off_s, frac_s, part_s,
):
    date, rng = lax.axis_index("date"), lax.axis_index("rng")
    planes = nx * nz
    nxy = nx * NY
    ts = TILES // nz
    plane, y = date // NY, date % NY
    z, xy = plane % nz, (plane // nz) * NY + y
    has_left, has_right = rng > 0, rng < nr - 1
    has_before, has_after = plane > 0, plane < planes - 1

    def z_date(k):
        return ((plane // nz) * nz + (z + k) % nz) * NY + y

    def xy_date(k):
        other = (xy + k) % nxy
        return ((other // NY) * nz + z) * NY + other % NY

    def remote(src, dst, send, recv, to_date, to_rng):
        return pltpu.make_async_remote_copy(
            src_ref=src, dst_ref=dst, send_sem=send, recv_sem=recv,
            device_id=(to_date, to_rng), device_id_type=MESH,
        )

    barrier = pltpu.get_barrier_semaphore()

    def hello(to_date, to_rng):
        pl.semaphore_signal(barrier, inc=1, device_id=(to_date, to_rng), device_id_type=MESH)

    for k in range(1, nz):
        hello(z_date(k), rng)
    for k in range(1, nxy):
        hello(xy_date(k), rng)
    for present, to_date, to_rng in (
        (has_left, date, rng - 1), (has_right, date, rng + 1),
        (has_before, date - NY, rng), (has_after, date + NY, rng),
    ):
        @pl.when(present)
        def _(to_date=to_date, to_rng=to_rng):
            hello(to_date, to_rng)

    loads = [
        pltpu.make_async_copy(slc_h.at[0, :, :, pl.ds(128 * p, 128)], samples.at[p], in_sem.at[p])
        for p in range(TILES)
    ]
    for load in loads:
        load.start()
    table_load = pltpu.make_async_copy(table_h, table, in_sem.at[TILES])
    table_load.start()
    scalars = [
        pltpu.make_async_copy(source, target, scalar_sem.at[i])
        for i, (source, target) in enumerate(((off_h, off_s), (frac_h, frac_s), (part_h, part_s), (ref_h, ref_s)))
    ]
    for copy in scalars:
        copy.start()

    lane = lax.broadcasted_iota(jnp.int32, (LANES, LANES), 1)
    diff = lax.broadcasted_iota(jnp.int32, (LANES, LANES), 0) - lane
    lane8 = lane[0:8]
    for copy in scalars:
        copy.wait()
    rows = tap_rows(off_s, frac_s)
    taps[...] = rows

    @pl.when(jnp.logical_not(has_left))
    def _():
        halo[0] = jnp.zeros((2, ROWS, LANES), BF16)
        tap_halo[0] = jnp.zeros((8, LANES), F32)

    @pl.when(jnp.logical_not(has_right))
    def _():
        halo[1] = jnp.zeros((2, ROWS, LANES), BF16)
        tap_halo[1] = jnp.zeros((8, LANES), F32)

    for h in range(1, SPAN + 1):
        @pl.when(jnp.logical_not(jnp.logical_or(y + h < NY, has_after)))
        def _(h=h):
            coh[h - 1] = jnp.zeros((ROWS, TILES * LANES), BF16)

    root = jnp.where(ref_s[0] == date, 1.0, 0.0).astype(F32)
    for p in range(TILES):
        loads[p].wait()
        real, imag = samples[p, 0].astype(F32), samples[p, 1].astype(F32)
        size = jnp.sqrt(real * real + imag * imag + 1e-06).astype(BF16)
        amp[p] = size
        masked[p] = (size.astype(F32) * root).astype(BF16)

    greeted = (nz - 1) + (nxy - 1)
    for present in (has_left, has_right, has_before, has_after):
        greeted = greeted + present.astype(jnp.int32)
    pl.semaphore_wait(barrier, greeted)

    scatters = []
    for k in range(1, nz):
        to = (z + k) % nz
        scatters.append(
            remote(masked.at[pl.ds(to * ts, ts)], scatter.at[k - 1], rs_send.at[k - 1], rs_recv.at[k - 1],
                   z_date(k), rng)
        )
    to_left = [
        remote(samples.at[0], halo.at[1], halo_send.at[0], halo_recv.at[0], date, rng - 1),
        remote(taps.at[pl.ds(0, 8)], tap_halo.at[1], halo_send.at[1], halo_recv.at[1], date, rng - 1),
    ]
    to_right = [
        remote(samples.at[7], halo.at[0], halo_send.at[2], halo_recv.at[2], date, rng + 1),
        remote(taps.at[pl.ds(8, 8)], tap_halo.at[0], halo_send.at[3], halo_recv.at[3], date, rng + 1),
    ]

    for copy in scatters:
        copy.start()

    @pl.when(has_left)
    def _():
        for copy in to_left:
            copy.start()

    @pl.when(has_right)
    def _():
        for copy in to_right:
            copy.start()

    chunks = ((2, 3), (5, 3), (0, 2))
    nc = len(chunks) + 1

    def item_copies(source, source_edge, slot, sends, to_date):
        copies = [
            remote(
                source.at[pl.ds(start, count)], partner.at[slot, pl.ds(start, count)],
                sends.at[c], item_recv.at[slot, c], to_date, rng,
            )
            for c, (start, count) in enumerate(chunks)
        ]
        copies.append(
            remote(source_edge, partner_edge.at[slot], sends.at[nc - 1], item_recv.at[slot, nc - 1], to_date, rng)
        )
        return copies

    own_dests = [(has_before, 3, date - NY), (y >= 1, 0, date - 1), (y >= 3, 2, date - 3)]
    own_copies = [item_copies(own, edge, slot, own_send.at[i], to) for i, (_, slot, to) in enumerate(own_dests)]
    middle = jnp.logical_and(y >= 1, y + 1 < NY)
    relay_dests = [
        (jnp.logical_and(has_after, y + 1 < NY), 3, 2, date + 1),
        (jnp.logical_and(has_after, y + 3 < NY), 3, 0, date + 3),
        (middle, 0, 1, date - 1),
        (jnp.logical_and(has_after, middle), 2, 1, date + 1),
    ]
    relay_copies = [
        item_copies(partner.at[source], partner_edge.at[source], slot, relay_send.at[i], to)
        for i, (_, source, slot, to) in enumerate(relay_dests)
    ]

    def arrived(slot, c):
        remote(
            edge if c == nc - 1 else own.at[pl.ds(*chunks[c])],
            partner_edge.at[slot] if c == nc - 1 else partner.at[slot, pl.ds(*chunks[c])],
            own_send.at[0, c], item_recv.at[slot, c], date, rng,
        ).wait_recv()

    def send_own(c, which):
        for i in which:
            @pl.when(own_dests[i][0])
            def _(i=i):
                own_copies[i][c].start()

    def store_own(s, keep=None):
        if s < TILES:
            first, second = rows[2 * s : 2 * s + 1], rows[2 * s + 1 : 2 * s + 2]
        else:
            first, second = tap_halo[1][0:1], tap_halo[0][7:8]
        tile = resample_tile(s, samples, first, second, lane, diff)
        if keep is not None:
            tile = jnp.where(keep, tile, 0.0)
            edge[...] = pack_edge(tile, lane).astype(BF16)
        own[at(s)] = tile.astype(BF16).reshape(2, ROWS, LANES)

    for s in range(1, 4):
        store_own(s)
    send_own(0, (0, 1, 2))
    for s in range(4, 7):
        store_own(s)
    send_own(1, (0, 1, 2))

    @pl.when(has_right)
    def _():
        to_left[0].wait_recv()
        to_left[1].wait_recv()

    @pl.when(has_left)
    def _():
        to_right[0].wait_recv()
        to_right[1].wait_recv()

    lane_h = lax.broadcasted_iota(jnp.int32, (2, ROWS, LANES), 2)
    samples[8] = jnp.where(lane_h < 64, halo[1].astype(F32), halo[0].astype(F32)).astype(BF16)
    low_edge = jnp.where(has_right, 64, 0)
    high_edge = jnp.where(has_left, 64, 128)
    store_own(7)
    store_own(8, jnp.logical_or(lane < low_edge, lane >= high_edge))
    store_own(0)
    send_own(2, (0, 1, 2))
    send_own(3, (0, 1, 2))

    for copy in scatters:
        copy.wait_recv()
    total = masked[pl.ds(z * ts, ts)].astype(F32)
    for k in range(nz - 1):
        total = total + scatter[k].astype(F32)
    merged[...] = total.astype(BF16)
    exchanges = [
        remote(merged, exchange.at[k - 1], ae_send.at[k - 1], ae_recv.at[k - 1], xy_date(k), rng)
        for k in range(1, nxy)
    ]
    for copy in exchanges:
        copy.start()

    table_load.wait()
    parts, own_energy = spectrum(amp, table, lane8)
    for p in range(TILES):
        own_spec[p] = parts[p]

    def relay(source, c):
        exists = {0: y + 1 < NY, 2: jnp.logical_and(has_after, y >= 1), 3: has_after}[source]

        @pl.when(exists)
        def _():
            arrived(source, c)

        for (present, at_slot, _, _), copies in zip(relay_dests, relay_copies):
            if at_slot == source:
                @pl.when(present)
                def _(copies=copies):
                    copies[c].start()

    for c in range(2):
        relay(0, c)
        relay(3, c)

    for s in range(9):
        real, imag = own[at(s), 0].astype(F32), own[at(s), 1].astype(F32)
        fields[s, 0:64] = (real * real + imag * imag).astype(BF16)
    box_own[...] = boxes(fields, 64, table)

    for copy in exchanges:
        copy.wait_recv()
    total = merged[...].astype(F32)
    for k in range(nxy - 1):
        total = total + exchange[k].astype(F32)
    ref_amp[pl.ds(z * ts, ts)] = total.astype(BF16)
    mine = ref_amp.at[pl.ds(z * ts, ts)]
    gathers = [
        remote(mine, mine, ag_send.at[k - 1], ag_recv.at[k - 1], z_date(k), rng) for k in range(1, nz)
    ]
    for copy in gathers:
        copy.start()

    for c in range(2, nc):
        relay(0, c)
        relay(3, c)
    for c in range(2):
        relay(2, c)

    def pair(h):
        slot = h - 1
        partner[slot, TILES] = unpack_edge(partner_edge[slot].astype(F32), lane).astype(BF16).reshape(2, ROWS, LANES)
        for s in range(9):
            own0, own1 = own[at(s), 0].astype(F32), own[at(s), 1].astype(F32)
            other0, other1 = partner[slot, at(s), 0].astype(F32), partner[slot, at(s), 1].astype(F32)
            fields[s, 0:64] = (own0 * other0 + own1 * other1).astype(BF16)
            fields[s, 64:128] = (own1 * other0 - own0 * other1).astype(BF16)
            fields[s, 128:192] = (other0 * other0 + other1 * other1).astype(BF16)
        weight = part_s[0, slot].astype(F32)
        box = boxes(fields, 192, table)
        re, im, power = box[0:64], box[64:128], box[128:192]
        coh[slot] = (weight * (re * re + im * im) / (box_own[...] * power + 1e-06)).astype(BF16)

    @pl.when(has_after)
    def _():
        pair(SPAN)

    @pl.when(y + 1 < NY)
    def _():
        pair(1)

    for c in range(2, nc):
        relay(2, c)

    @pl.when(y + 3 < NY)
    def _():
        for c in range(nc):
            arrived(2, c)
        pair(3)

    @pl.when(jnp.logical_and(has_after, y >= 1))
    def _():
        pair(3)

    @pl.when(jnp.logical_and(has_after, y + 1 >= NY))
    def _():
        for c in range(nc):
            arrived(0, c)
        pair(1)

    for copy in gathers:
        copy.wait_recv()
    ref_parts, ref_energy = spectrum(ref_amp, table, lane8)
    surfaces(own_spec, own_energy, ref_parts, ref_energy, table, surf, lane8)

    @pl.when(jnp.logical_or(y + 2 < NY, has_after))
    def _():
        for c in range(nc):
            arrived(1, c)
        pair(2)

    for copy in scatters + exchanges + gathers:
        copy.wait_send()

    @pl.when(has_left)
    def _():
        for copy in to_left:
            copy.wait_send()

    @pl.when(has_right)
    def _():
        for copy in to_right:
            copy.wait_send()

    for dests, copies in ((own_dests, own_copies), (relay_dests, relay_copies)):
        for (present, *_), mine in zip(dests, copies):
            @pl.when(present)
            def _(mine=mine):
                for copy in mine:
                    copy.wait_send()


def write_kernel(surf, coh, surf_h, coh_h, rows, sem):
    large = pltpu.make_async_copy(coh, coh_h.at[0], sem.at[0])
    large.start()
    for q in range(8):
        rows[:, 128 * q : 128 * q + 128] = surf[:, q, :]
    small = pltpu.make_async_copy(rows, surf_h.at[0, 0], sem.at[1])
    small.start()
    large.wait()
    small.wait()


def body(nz, nx, nr, slc, ref_date, int_offset, frac_offset, partners):
    ts = TILES // nz
    nxy = nx * NY
    anywhere = pl.BlockSpec(memory_space=pl.ANY)
    vmem = pl.BlockSpec(memory_space=pltpu.VMEM)
    dma = pltpu.SemaphoreType.DMA
    tile = (2, ROWS, LANES)
    slab = (TILES, ROWS, LANES)
    surface, coherence = pl.pallas_call(
        functools.partial(kernel, nz, nx, nr),
        out_shape=(
            pltpu.VMEM((16, 8, LANES), F32),
            pltpu.VMEM((SPAN, ROWS, TILES * LANES), BF16),
        ),
        in_specs=[anywhere] * 6,
        out_specs=(vmem, vmem),
        scratch_shapes=[
            pltpu.VMEM((TABLE_ROWS, 256), BF16),
            pltpu.VMEM((9,) + tile, BF16),
            pltpu.VMEM((2,) + tile, BF16),
            pltpu.VMEM((16, LANES), F32),
            pltpu.VMEM((2, 8, LANES), F32),
            pltpu.VMEM(slab, BF16),
            pltpu.VMEM(slab, BF16),
            pltpu.VMEM((max(nz - 1, 1), ts, ROWS, LANES), BF16),
            pltpu.VMEM((ts, ROWS, LANES), BF16),
            pltpu.VMEM((nxy - 1, ts, ROWS, LANES), BF16),
            pltpu.VMEM(slab, BF16),
            pltpu.VMEM((TILES, 128, LANES), F32),
            pltpu.VMEM((9,) + tile, BF16),
            pltpu.VMEM((32, LANES), BF16),
            pltpu.VMEM((SPAN, 9) + tile, BF16),
            pltpu.VMEM((SPAN, 32, LANES), BF16),
            pltpu.VMEM((9, 192, LANES), BF16),
            pltpu.VMEM((ROWS, TILES * LANES), F32),
            dma((TILES + 1,)),
            dma((4,)), dma((4,)),
            dma((max(nz - 1, 1),)), dma((max(nz - 1, 1),)),
            dma((nxy - 1,)), dma((nxy - 1,)),
            dma((max(nz - 1, 1),)), dma((max(nz - 1, 1),)),
            dma((3, 4)), dma((4, 4)), dma((4, 4)), dma((4,)),
            pltpu.SMEM((1,), jnp.int32), pltpu.SMEM((1, 1, 16), jnp.int32),
            pltpu.SMEM((1, 1, 16), F32), pltpu.SMEM((1, SPAN), jnp.int32),
        ],
        compiler_params=pltpu.CompilerParams(collective_id=0, has_side_effects=True),
    )(ref_date, int_offset, frac_offset, partners, slc, tables())
    return pl.pallas_call(
        write_kernel,
        out_shape=(
            jax.ShapeDtypeStruct((1, 1, 16, 1024), F32),
            jax.ShapeDtypeStruct((1, SPAN, ROWS, TILES * LANES), BF16),
        ),
        in_specs=[vmem, vmem],
        out_specs=(anywhere, anywhere),
        scratch_shapes=[pltpu.VMEM((16, 1024), F32), dma((2,))],
    )(*(pltpu.with_memory_space_constraint(x, pltpu.VMEM) for x in (surface, coherence)))


def solution(mesh):
    dates, nr = mesh.shape["date"], mesh.shape["rng"]
    planes = dates // NY
    nz = min(planes, 8)
    in_specs = (
        P("date", None, None, "rng"),
        P(),
        P("date", None, "rng"),
        P("date", None, "rng"),
        P("date", None),
    )
    out_specs = (P("date", None, "rng", None), P("date", None, None, "rng"))
    return jax.shard_map(
        functools.partial(body, nz, planes // nz, nr),
        mesh=mesh, in_specs=in_specs, out_specs=out_specs, check_vma=False,
    )
```
